32 devices in a mesh: grp: 2 (over y), seq: 4 (over z), head: 4 (over x, core).
Axes of the slice: x: 2, y: 2, z: 4, core: 2. Of those that a mesh axis runs over, the one named last changes fastest.
Arguments:
- lin_q: bfloat16 [1024, 2048], P(('grp', 'seq'), 'head'), parts along dimension 0, may hold values from -6 to 6
- lin_k: bfloat16 [1024, 2048], P(('grp', 'seq'), 'head'), parts along dimension 0, may hold values from -6 to 6
- lin_v: bfloat16 [1024, 4096], P(('grp', 'seq'), 'head'), parts along dimension 0, may hold values from -6 to 6
- conv_q: bfloat16 [4, 2048], P(None, 'head'), may hold values from -3 to 3
- conv_k: bfloat16 [4, 2048], P(None, 'head'), may hold values from -3 to 3
- conv_v: bfloat16 [4, 4096], P(None, 'head'), may hold values from -3 to 3
- lin_z: bfloat16 [1024, 4096], P(('grp', 'seq'), 'head'), parts along dimension 0, may hold values from -6 to 6
- beta_logit: float32 [1024, 32], P(('grp', 'seq'), 'head'), parts along dimension 0, may hold values from -7 to 2
- log_decay: float32 [1024, 32], P(('grp', 'seq'), 'head'), parts along dimension 0, may hold values from -1.1 to 0
- attn_query: bfloat16 [1024, 4096], P(('grp', 'seq'), 'head'), parts along dimension 0, may hold values from -6 to 6
- attn_gate: bfloat16 [1024, 4096], P(('grp', 'seq'), 'head'), parts along dimension 0, may hold values from -6 to 6
- attn_kv: bfloat16 [1024, 2, 2, 256], P(('grp', 'seq')), parts along dimension 0, may hold values from -6 to 6
- doc_lengths: int32 [10], P('grp'), parts along dimension 0, may hold values from 1 to 128, 512 in all
Outputs:
- delta_out: bfloat16 [1024, 4096], P(('grp', 'seq'), 'head'), parts along dimension 0
- attn_out: bfloat16 [1024, 4096], P(('grp', 'seq'), 'head'), parts along dimension 0
The draws below stay inside these ranges and needn't reach their ends.
There are 2 independent parts, one for each index of `grp`. The reference program is written for one: setup_inputs(seed, part) draws one part's arguments, and reference() takes and returns one part's arrays. A program takes and returns all parts, laid end to end along the dimension named above; an argument that names none is the same for every part. Nothing has to cross between parts.
Inputs may be any that keep to these rules, and one draw needn't show every extreme that they name: `doc_lengths`: the 5 documents packed in order into the slab; their lengths sum to 512.
All inputs are finite; a program needn't handle non-finite values.
Results may differ from the reference program's by a relative error of at most 0.0037.
Values may be sent and summed in bfloat16 or wider, within the bound.
A program may use at most 192 MiB of HBM per device.

```python
import math
import jax
import jax.numpy as jnp
import numpy as np
from jax import lax

DK = 128
DV = 128
QKH = 16
VALUE_HEADS = 32
CONV = 4
AQ = 16
KVH = 2
AD = 256
DOCS = 5
TOK_DEV = 128
SLAB_TOKENS = 512


def head_pace(key):
    chance = 0.5
    return jax.random.bernoulli(jax.random.fold_in(key, 11), chance, (VALUE_HEADS,))


def log_range(key, shape, lowest, highest):
    return jnp.exp(jax.random.uniform(key, shape, jnp.float32, math.log(lowest), math.log(highest)))


def draw_log_decay(key, part):
    slow_heads = head_pace(key)
    random_key_split = jax.random.split(jax.random.fold_in(key, 23), 6)
    fast_rate = log_range(random_key_split[0], (VALUE_HEADS,), 0.03, 0.1)
    slow_rate = log_range(random_key_split[1], (VALUE_HEADS,), 0.05, 0.3) / SLAB_TOKENS
    head_decay_rate = jnp.where(slow_heads, slow_rate, fast_rate)
    block_count = SLAB_TOKENS // TOK_DEV
    block_multiplier = jnp.repeat(log_range(random_key_split[2], (block_count, VALUE_HEADS), 0.5, 2.0), TOK_DEV, axis=0)
    token_multiplier = log_range(random_key_split[3], (SLAB_TOKENS, VALUE_HEADS), 0.5, 2.0)
    group_rows = jax.random.randint(random_key_split[4], (2,), 0, SLAB_TOKENS)
    group_length = jax.random.uniform(random_key_split[5], (2, VALUE_HEADS), jnp.float32, 0.22, 0.69)
    matched_rows = (jnp.arange(SLAB_TOKENS)[:, None] == group_rows[None, :]).astype(jnp.float32)
    row_groups = jnp.sum(matched_rows[:, :, None] * group_length[None, :, :], axis=1)
    return -(head_decay_rate[None, :] * block_multiplier * token_multiplier) - row_groups


def draw_beta_logit(key, part):
    slow_heads = head_pace(key)
    lowest = jnp.where(slow_heads, -7.0, -2.5)
    highest = jnp.where(slow_heads, -4.5, 2.0)
    fraction = jax.random.uniform(jax.random.fold_in(key, 31), (SLAB_TOKENS, VALUE_HEADS), jnp.float32)
    return lowest[None, :] + (highest - lowest)[None, :] * fraction


def draw_attn_query(key, part):
    base_key = jax.random.fold_in(key, 43)
    drawn = jnp.clip(jax.random.normal(base_key, (SLAB_TOKENS, AQ * AD), jnp.float32), -6.0, 6.0)
    return drawn.astype(jnp.bfloat16)


def draw_attn_kv(key, part):
    base_key = jax.random.fold_in(key, 53)
    drawn = jnp.clip(jax.random.normal(base_key, (SLAB_TOKENS, 2, KVH, AD), jnp.float32), -6.0, 6.0)
    return drawn.astype(jnp.bfloat16)


def block_scale(key, shape, pieces, least, top_value):
    def one(axis_at, blocks):
        steps = jax.random.uniform(jax.random.fold_in(jax.random.fold_in(key, 6), axis_at), (blocks,), jnp.float32, least / len(pieces), top_value / len(pieces))
        return jnp.repeat(jnp.exp(steps), shape[axis_at] // blocks).reshape((-1,) + (1,) * (len(shape) - axis_at - 1))

    loudness = one(*pieces[0])
    for cut in pieces[1:]:
        loudness = loudness * one(*cut)
    return loudness


def profile(amount, total, reach, lean):
    loads = [(1 << 20) // math.isqrt(grade ** lean) + 1 for grade in range(2, amount + 1)]
    rest, holding = total - reach - (amount - 1), [1] * (amount - 1)
    while rest > 0:
        candidates = [i for i in range(amount - 1) if holding[i] < reach]
        pool, remaining = sum([loads[i] for i in candidates]), rest
        for i in candidates:
            extra = min(reach - holding[i], max(1, remaining * loads[i] // pool), rest)
            holding[i] = holding[i] + extra
            rest = rest - extra
    return np.array([reach] + holding)


def ragged_sizes(key, count, total, limit, skew):
    if count == 2:
        one = jax.random.randint(key, (), max(1, total - limit), min(limit, total - 1) + 1)
        return jnp.stack([one, total - one])
    sizes = jnp.asarray(profile(count, total, limit, skew), jnp.int32)
    couples = (count - 1) // 2
    source_of, receiver = sizes[1:1 + 2 * couples:2], sizes[2:2 + 2 * couples:2]
    room = jnp.minimum(source_of - 1, limit - receiver)
    shifted = jax.random.randint(jax.random.fold_in(key, 1), (couples,), 0, 1 << 20) % (room + 1)
    sizes = sizes.at[1:1 + 2 * couples:2].set(source_of - shifted).at[2:2 + 2 * couples:2].set(receiver + shifted)
    return sizes[jax.random.permutation(jax.random.fold_in(key, 2), count)]


def gaussian(rng, dims, width, limit, shards=(), kind=jnp.bfloat16):
    loudness = block_scale(rng, dims, shards, -0.22, 0.18) if shards else 1.0
    entries = jax.random.normal(rng, dims, jnp.float32) * width * loudness
    return jnp.minimum(jnp.maximum(entries, -limit), limit).astype(kind)


def setup_inputs(seed: int = 0, part: int = 0) -> dict:
    arg_keys = jax.random.split(jax.random.key(seed), 14)
    own_keys = jax.random.split(jax.random.fold_in(arg_keys[13], part), 14)
    lin_q = gaussian(own_keys[0], (SLAB_TOKENS, QKH * DK), 1.0, 6.0, ((0, 4), (1, 4)))
    lin_k = gaussian(own_keys[1], (SLAB_TOKENS, QKH * DK), 1.0, 6.0, ((0, 4), (1, 4)))
    lin_v = gaussian(own_keys[2], (SLAB_TOKENS, VALUE_HEADS * DV), 1.0, 6.0, ((0, 4), (1, 4)))
    conv_q = gaussian(arg_keys[3], (CONV, QKH * DK), CONV ** -0.5, 3.0, ((1, 4),))
    conv_k = gaussian(arg_keys[4], (CONV, QKH * DK), CONV ** -0.5, 3.0, ((1, 4),))
    conv_v = gaussian(arg_keys[5], (CONV, VALUE_HEADS * DV), CONV ** -0.5, 3.0, ((1, 4),))
    lin_z = gaussian(own_keys[6], (SLAB_TOKENS, VALUE_HEADS * DV), 1.0, 6.0, ((0, 4), (1, 4)))
    beta_logit = draw_beta_logit(jax.random.fold_in(jax.random.fold_in(arg_keys[13], part), 71), part)
    log_decay = draw_log_decay(jax.random.fold_in(jax.random.fold_in(arg_keys[13], part), 71), part)
    attn_query = draw_attn_query(jax.random.fold_in(jax.random.fold_in(arg_keys[13], part), 71), part)
    attn_gate = gaussian(own_keys[10], (SLAB_TOKENS, AQ * AD), 1.0, 6.0, ((0, 4), (1, 4)))
    attn_kv = draw_attn_kv(jax.random.fold_in(jax.random.fold_in(arg_keys[13], part), 71), part)
    doc_lengths = ragged_sizes(own_keys[12], DOCS, SLAB_TOKENS, SLAB_TOKENS // 4, 0).astype(jnp.int32)
    return {"lin_q": lin_q, "lin_k": lin_k, "lin_v": lin_v, "conv_q": conv_q, "conv_k": conv_k, "conv_v": conv_v, "lin_z": lin_z, "beta_logit": beta_logit, "log_decay": log_decay, "attn_query": attn_query, "attn_gate": attn_gate, "attn_kv": attn_kv, "doc_lengths": doc_lengths}


EXACT_PRECISION = lax.Precision.HIGHEST
NEGATIVE = -1e+30

def segment_ids(positions, doc_lengths):
    offsets = jnp.cumsum(doc_lengths) - doc_lengths
    return lax.optimization_barrier(jnp.sum((offsets[None, :] <= positions[:, None]).astype(jnp.int32), axis=1))

def start_flags(positions, doc_lengths):
    offsets = jnp.cumsum(doc_lengths) - doc_lengths
    return jnp.any(offsets[None, :] == positions[:, None], axis=1)

def causal_conv(values, weights, positions, segment, doc_lengths):
    row_count = values.shape[0]
    tap_count = weights.shape[0]
    padding = jnp.zeros((tap_count - 1, values.shape[1]), jnp.float32)
    extended = jnp.concatenate([padding, values.astype(jnp.float32)], axis=0)
    conv_sum = jnp.zeros(values.shape, jnp.float32)
    for tap_index in range(tap_count):
        source = positions - (tap_count - 1) + tap_index
        inside = (segment_ids(source, doc_lengths) == segment).astype(jnp.float32)
        conv_sum = conv_sum + extended[tap_index:tap_index + row_count] * weights[tap_index].astype(jnp.float32)[None, :] * inside[:, None]
    return jax.nn.silu(conv_sum)

def unit_heads(values, head_size):
    shaped = values.reshape(values.shape[0], -1, head_size)
    return shaped * lax.rsqrt(lax.optimization_barrier(jnp.sum(shaped * shaped, axis=-1, keepdims=True)) + 1e-06)

def reference(lin_q, lin_k, lin_v, conv_q, conv_k, conv_v, lin_z, beta_logit, log_decay, attn_query, attn_gate, attn_kv, doc_lengths):
    positions = jnp.arange(SLAB_TOKENS, dtype=jnp.int32)
    segment = segment_ids(positions, doc_lengths)
    starts = start_flags(positions, doc_lengths)
    queries = unit_heads(causal_conv(lin_q, conv_q, positions, segment, doc_lengths), DK) * DK ** (-0.5)
    keys_unit = unit_heads(causal_conv(lin_k, conv_k, positions, segment, doc_lengths), DK)
    values = causal_conv(lin_v, conv_v, positions, segment, doc_lengths).reshape(SLAB_TOKENS, VALUE_HEADS, DV)
    queries = jnp.repeat(queries, VALUE_HEADS // QKH, axis=1)
    keys_unit = jnp.repeat(keys_unit, VALUE_HEADS // QKH, axis=1)
    beta_gate = jax.nn.sigmoid(beta_logit)
    decay_rates = jnp.exp(log_decay) * (1.0 - starts.astype(jnp.float32))[:, None]

    def advance(recurrent_state, inputs):
        query_transposed, key_transposed, value_t, beta_t, rate_t = inputs
        projected_input = jnp.einsum('bg,bgm->bm', key_transposed, recurrent_state, precision=EXACT_PRECISION)
        recurrent_state = rate_t[:, None, None] * (recurrent_state - beta_t[:, None, None] * key_transposed[:, :, None] * projected_input[:, None, :]) + beta_t[:, None, None] * key_transposed[:, :, None] * value_t[:, None, :]
        return (recurrent_state, jnp.einsum('bg,bgm->bm', query_transposed, recurrent_state, precision=EXACT_PRECISION))
    _, delta_output = lax.scan(advance, jnp.zeros((VALUE_HEADS, DK, DV), jnp.float32), (queries, keys_unit, values, beta_gate, decay_rates))
    inverse_rms = lax.rsqrt(lax.optimization_barrier(jnp.mean(delta_output * delta_output, axis=-1, keepdims=True)) + 1e-06)
    gate_z = jax.nn.silu(lin_z.astype(jnp.float32).reshape(SLAB_TOKENS, VALUE_HEADS, DV))
    delta_out = (delta_output * inverse_rms * gate_z).astype(jnp.bfloat16).reshape(SLAB_TOKENS, VALUE_HEADS * DV)
    query_all = attn_query.reshape(SLAB_TOKENS, KVH, AQ // KVH, AD).astype(jnp.float32)
    key_all = attn_kv[:, 0].astype(jnp.float32)
    value_all = attn_kv[:, 1].astype(jnp.float32)
    span_rows = math.gcd(SLAB_TOKENS, 256)

    def one_span(span_index):
        first_row = (span_index * span_rows).astype(jnp.int32)
        query_part = lax.dynamic_slice_in_dim(query_all, first_row, span_rows, 0)
        query_pos = first_row + jnp.arange(span_rows, dtype=jnp.int32)
        query_seg = lax.dynamic_slice_in_dim(segment, first_row, span_rows, 0)
        allowed = (positions[None, :] <= query_pos[:, None]) & (segment[None, :] == query_seg[:, None])
        scores = jnp.einsum('qcgd,kcd->cgqk', query_part, key_all, precision=EXACT_PRECISION) * AD ** (-0.5)
        masked = jnp.where(allowed, scores, NEGATIVE)
        row_top = lax.optimization_barrier(jnp.max(masked, axis=-1, keepdims=True))
        weights_f = jnp.where(allowed, jnp.exp(masked - row_top), 0.0)
        row_total = lax.optimization_barrier(jnp.sum(weights_f, axis=-1))
        rounded = lax.optimization_barrier(weights_f.astype(jnp.bfloat16)).astype(jnp.float32)
        mixture = jnp.einsum('cgqk,kcd->qcgd', rounded, value_all, precision=EXACT_PRECISION)
        mixture = mixture / jnp.transpose(row_total, (2, 0, 1))[..., None]
        return mixture.reshape(span_rows, AQ * AD)
    attended = lax.map(one_span, jnp.arange(SLAB_TOKENS // span_rows, dtype=jnp.int32)).reshape(SLAB_TOKENS, AQ * AD)
    attn_out = (attended * jax.nn.sigmoid(attn_gate.astype(jnp.float32))).astype(jnp.bfloat16)
    return (delta_out, attn_out)
```

```python
import functools

import jax
import jax.numpy as jnp
from jax import lax
from jax.experimental import pallas as pl
from jax.experimental.pallas import tpu as pltpu
from jax.sharding import PartitionSpec as P

DK = 128
DV = 128
QKH = 16
VALUE_HEADS = 32
AQ = 16
KVH = 2
AD = 256
BLOCK = 64


EXACT_PRECISION = lax.Precision.HIGHEST
NEGATIVE = -1e30


def passed_along(value, axis, steps):
    count = lax.axis_size(axis)
    initial, last = (max(0, -steps), min(count, count - steps))
    return lax.ppermute(value, axis, [(source, source + steps) for source in range(initial, last)])


def prefix_2(value, axis, combine, identity):
    length, index = (lax.axis_size(axis), lax.axis_index(axis))
    everything = jax.tree.map(
        lambda part, kind: lax.all_gather(part.astype(kind), axis),
        value,
        (jnp.bfloat16, jnp.bfloat16),
    )
    start = jax.tree.map(
        lambda part, zero: jnp.broadcast_to(jnp.asarray(zero, part.dtype), part.shape),
        value,
        identity,
    )

    def step(k, before):
        reached = k < index
        new = combine(
            before, jax.tree.map(lambda part, own: part[k].astype(own.dtype), everything, value)
        )
        return jax.tree.map(lambda a, b: jnp.where(reached, a, b), new, before)

    return lax.fori_loop(0, length, step, start)


def segment_ids(positions, doc_lengths):
    offsets = jnp.cumsum(doc_lengths) - doc_lengths
    return jnp.sum((offsets[None, :] <= positions[:, None]).astype(jnp.int32), axis=1)


def start_flags(positions, doc_lengths):
    offsets = jnp.cumsum(doc_lengths) - doc_lengths
    return jnp.any(offsets[None, :] == positions[:, None], axis=1)


def causal_conv(values, margin, weights, positions, segment, doc_lengths):
    row_count = values.shape[0]
    tap_count = weights.shape[0]
    extended = jnp.concatenate([margin, values], axis=0).astype(jnp.float32)
    conv_sum = jnp.zeros(values.shape, jnp.float32)
    for tap_index in range(tap_count):
        source = positions - (tap_count - 1) + tap_index
        inside = (segment_ids(source, doc_lengths) == segment).astype(jnp.float32)
        conv_sum = (
            conv_sum
            + extended[tap_index : tap_index + row_count]
            * weights[tap_index].astype(jnp.float32)[None, :]
            * inside[:, None]
        )
    return jax.nn.silu(conv_sum)


def unit_heads(values, head_size):
    shaped = values.reshape(values.shape[0], -1, head_size)
    return shaped * lax.rsqrt(jnp.sum(shaped * shaped, axis=-1, keepdims=True) + 1e-06)


def compose(first_pair, second_pair):
    joined_map = jnp.einsum(
        "hij,hjk->hik", second_pair[0], first_pair[0], precision=EXACT_PRECISION
    )
    joined_shift = (
        jnp.einsum("hij,hjk->hik", second_pair[0], first_pair[1], precision=EXACT_PRECISION)
        + second_pair[1]
    )
    return (joined_map, joined_shift)


def unit_lower_inverse(lower_part, block_len):
    identity = jnp.eye(block_len, dtype=jnp.float32)
    power = -lower_part
    inverse = identity + power
    for _ in range(max(block_len - 1, 1).bit_length() - 1):
        power = jnp.einsum("nhij,nhjk->nhik", power, power, precision=EXACT_PRECISION)
        inverse = jnp.einsum(
            "nhij,nhjk->nhik", inverse, identity + power, precision=EXACT_PRECISION
        )
    return inverse


def delta_blocks(queries, keys_unit, values, beta_gate, log_rates, segment, starts):
    row_count, head_count, key_size = keys_unit.shape
    value_size = values.shape[2]
    block_len = BLOCK
    block_count = row_count // block_len

    def to_blocks(array):
        return jnp.swapaxes(array.reshape((block_count, block_len) + array.shape[1:]), 1, 2)

    query_blk = to_blocks(queries)
    key_blk = to_blocks(keys_unit)
    value_blk = to_blocks(values)
    beta_blk = to_blocks(beta_gate)
    cumulative = jnp.cumsum(to_blocks(log_rates), axis=-1)
    segment_blk = segment.reshape(block_count, block_len)
    fresh_count = jnp.cumsum(starts.reshape(block_count, block_len).astype(jnp.int32), axis=-1)
    later_row = lax.broadcasted_iota(jnp.int32, (block_len, block_len), 0)
    earlier_col = lax.broadcasted_iota(jnp.int32, (block_len, block_len), 1)
    visible = (later_row >= earlier_col)[None] & (
        segment_blk[:, :, None] == segment_blk[:, None, :]
    )
    visible = visible[:, None]
    spread = cumulative[..., :, None] - cumulative[..., None, :]
    decay_mat = jnp.where(visible, jnp.exp(jnp.where(visible, spread, 0.0)), 0.0)
    carried = jnp.where((fresh_count == 0)[:, None, :], jnp.exp(cumulative), 0.0)
    key_key = jnp.einsum("nhik,nhjk->nhij", key_blk, key_blk, precision=EXACT_PRECISION)
    strict = (later_row > earlier_col).astype(jnp.float32)
    lower_part = decay_mat * strict * key_key * beta_blk[..., None, :]
    inverse = unit_lower_inverse(lower_part, block_len)
    right_side = jnp.concatenate([value_blk, carried[..., None] * key_blk], axis=-1)
    solved = jnp.einsum("nhij,nhjc->nhic", inverse, right_side, precision=EXACT_PRECISION)
    moved_values = solved[..., :value_size]
    moved_keys = solved[..., value_size:]
    query_key = jnp.einsum("nhik,nhjk->nhij", query_blk, key_blk, precision=EXACT_PRECISION)
    attend = decay_mat * query_key * beta_blk[..., None, :]
    out_zero = jnp.einsum("nhij,nhjv->nhiv", attend, moved_values, precision=EXACT_PRECISION)
    reach_part = carried[..., None] * query_blk - jnp.einsum(
        "nhij,nhjk->nhik", attend, moved_keys, precision=EXACT_PRECISION
    )
    weighted = (beta_blk * decay_mat[..., block_len - 1, :])[..., None] * key_blk
    block_map = carried[..., block_len - 1][..., None, None] * jnp.eye(
        key_size, dtype=jnp.float32
    ) - jnp.einsum("nhjk,nhjl->nhkl", weighted, moved_keys, precision=EXACT_PRECISION)
    block_shift = jnp.einsum("nhjk,nhjv->nhkv", weighted, moved_values, precision=EXACT_PRECISION)

    def advance(prefix, current):
        return (compose(prefix, current), prefix)

    eye_heads = jnp.broadcast_to(
        jnp.eye(key_size, dtype=jnp.float32), (head_count, key_size, key_size)
    )
    zero_heads = jnp.zeros((head_count, key_size, value_size), jnp.float32)
    device_pair, prefixes = lax.scan(advance, (eye_heads, zero_heads), (block_map, block_shift))
    baseline_output = out_zero + jnp.einsum(
        "nhik,nhkv->nhiv", reach_part, prefixes[1], precision=EXACT_PRECISION
    )
    complete_reach = jnp.einsum(
        "nhik,nhkl->nhil", reach_part, prefixes[0], precision=EXACT_PRECISION
    )
    return (device_pair, baseline_output, complete_reach, eye_heads, zero_heads)


def shards(
    lin_q,
    lin_k,
    lin_v,
    conv_q,
    conv_k,
    conv_v,
    lin_z,
    beta_logit,
    log_decay,
    attn_query,
    attn_gate,
    attn_kv,
    doc_lengths,
):
    row_count = lin_q.shape[0]
    seq_index = lax.axis_index("seq")
    positions = seq_index * row_count + jnp.arange(row_count, dtype=jnp.int32)
    segment = segment_ids(positions, doc_lengths)
    starts = start_flags(positions, doc_lengths)
    rim_from = row_count - conv_q.shape[0] + 1
    rim_q, rim_k, rim_v = passed_along(
        (lin_q[rim_from:], lin_k[rim_from:], lin_v[rim_from:]), "seq", 1
    )
    queries = unit_heads(
        causal_conv(lin_q, rim_q, conv_q, positions, segment, doc_lengths), DK
    ) * DK ** (-0.5)
    keys_unit = unit_heads(causal_conv(lin_k, rim_k, conv_k, positions, segment, doc_lengths), DK)
    values = causal_conv(lin_v, rim_v, conv_v, positions, segment, doc_lengths).reshape(
        row_count, -1, DV
    )
    head_count = values.shape[1]
    queries = jnp.repeat(queries, VALUE_HEADS // QKH, axis=1)
    keys_unit = jnp.repeat(keys_unit, VALUE_HEADS // QKH, axis=1)
    beta_gate = jax.nn.sigmoid(beta_logit)
    device_pair, baseline_output, complete_reach, eye_heads, zero_heads = delta_blocks(
        queries, keys_unit, values, beta_gate, log_decay, segment, starts
    )
    arriving_input = prefix_2(
        (device_pair[0], device_pair[1]), "seq", compose, (eye_heads, zero_heads)
    )
    delta_output = baseline_output + jnp.einsum(
        "dpjt,ptw->dpjw", complete_reach, arriving_input[1], precision=EXACT_PRECISION
    )
    delta_output = jnp.swapaxes(delta_output, 1, 2).reshape(row_count, head_count, DV)
    inverse_rms = lax.rsqrt(jnp.mean(delta_output * delta_output, axis=-1, keepdims=True) + 1e-06)
    gate_z = jax.nn.silu(lin_z.astype(jnp.float32).reshape(row_count, head_count, DV))
    delta_out = (
        (delta_output * inverse_rms * gate_z)
        .astype(jnp.bfloat16)
        .reshape(row_count, head_count * DV)
    )
    aq_local = attn_query.shape[1] // AD
    query_heads = attn_query.reshape(row_count, aq_local, AD)
    kv_head = lax.axis_index("head") * aq_local // (AQ // KVH)
    own_pair = lax.dynamic_index_in_dim(attn_kv, kv_head, axis=2, keepdims=False)
    score_scale = AD ** (-0.5)

    def absorb(running, kv_piece, first_row):
        row_top, row_total, accum = running
        piece_rows = kv_piece.shape[0]
        key_pos = first_row + jnp.arange(piece_rows, dtype=jnp.int32)
        key_seg = segment_ids(key_pos, doc_lengths)
        allowed = (
            (key_pos[None, :] <= positions[:, None])
            & (key_seg[None, :] == segment[:, None])
            & (key_pos[None, :] >= 0)
        )
        scores = (
            jnp.einsum(
                "qhd,kd->hqk", query_heads, kv_piece[:, 0], preferred_element_type=jnp.float32
            )
            * score_scale
        )
        masked = jnp.where(allowed[None], scores, NEGATIVE)
        new_top = jnp.maximum(row_top, jnp.max(masked, axis=-1))
        weights_f = jnp.where(allowed[None], jnp.exp(masked - new_top[..., None]), 0.0)
        rescale = jnp.exp(row_top - new_top)
        row_total = row_total * rescale + jnp.sum(weights_f, axis=-1)
        accum = accum * rescale[..., None] + jnp.einsum(
            "hqk,kd->hqd",
            weights_f.astype(jnp.bfloat16),
            kv_piece[:, 1],
            preferred_element_type=jnp.float32,
        )
        return (new_top, row_total, accum)

    start_state = (
        jnp.full((aq_local, row_count), NEGATIVE, jnp.float32),
        jnp.zeros((aq_local, row_count), jnp.float32),
        jnp.zeros((aq_local, row_count, AD), jnp.float32),
    )
    running = absorb(start_state, own_pair, seq_index * row_count)

    def hop(hop_step, loop_state):
        loop_running, kv_piece = loop_state
        kv_piece = passed_along(kv_piece, "seq", 1)
        loop_running = absorb(loop_running, kv_piece, (seq_index - hop_step - 1) * row_count)
        return (loop_running, kv_piece)

    running, _ = lax.fori_loop(0, lax.axis_size("seq") // 4, hop, (running, own_pair))
    row_top, row_total, accum = running
    attended = jnp.swapaxes(accum / row_total[..., None], 0, 1).reshape(row_count, aq_local * AD)
    attn_out = (attended * jax.nn.sigmoid(attn_gate.astype(jnp.float32))).astype(jnp.bfloat16)
    return (delta_out, attn_out)


BF = jnp.bfloat16
F32 = jnp.float32
LANES = 128
GROUPS = 2


def mm(a, b, transposed=False):
    contract = ((1,), (1,)) if transposed else ((1,), (0,))
    return lax.dot_general(a, b, (contract, ((), ())), preferred_element_type=F32)


def halves(x):
    high = x.astype(BF)
    return high, (x - high.astype(F32)).astype(BF)


def lhs3(x):
    high, low = halves(x)
    return jnp.concatenate([high, low, high], axis=1)


def rhs3(x):
    high, low = halves(x)
    return jnp.concatenate([high, high, low], axis=0)


def fused_kernel(
    count,
    doc_ref,
    lin_q,
    lin_k,
    lin_v,
    conv_q,
    conv_k,
    conv_v,
    lin_z,
    beta_logit,
    log_decay,
    attn_query,
    attn_gate,
    kv_own,
    delta_out,
    attn_out,
    rim_q,
    rim_k,
    rim_v,
    kv_before,
    state_out,
    state_in,
    spread_q,
    spread_k,
    spread_v,
    packed,
    local_out,
    reach_out,
    send_sem,
    recv_sem,
):
    rows = lin_q.shape[0]
    heads = lin_v.shape[1] // DV
    shared = heads // (lin_k.shape[1] // DK)
    docs = doc_ref.shape[0]
    rim = rim_q.shape[0]
    index = lax.axis_index("seq")
    barrier = pltpu.get_barrier_semaphore()

    def transfer(source, target, slot):
        return pltpu.make_async_remote_copy(
            src_ref=source,
            dst_ref=target,
            send_sem=send_sem.at[slot],
            recv_sem=recv_sem.at[slot],
            device_id={"seq": index + 1},
            device_id_type=pl.DeviceIdType.MESH,
        )

    tail = pl.ds(rows - rim, rim)
    early = [
        transfer(lin_k.at[tail, :], rim_k, 0),
        transfer(lin_v.at[tail, :], rim_v, 1),
        transfer(lin_q.at[tail, :], rim_q, 2),
        transfer(kv_own, kv_before, 3),
    ]
    per_group = heads // GROUPS
    states = [
        transfer(
            state_out.at[pl.ds(g * per_group, per_group)],
            state_in.at[pl.ds(g * per_group, per_group)],
            4 + g,
        )
        for g in range(GROUPS)
    ]

    @pl.when(index > 0)
    def _():
        pl.semaphore_signal(
            barrier, inc=1, device_id={"seq": index - 1}, device_id_type=pl.DeviceIdType.MESH
        )

    @pl.when(index < count - 1)
    def _():
        pl.semaphore_wait(barrier, 1)
        for copy in early:
            copy.start()

    @pl.when(index == 0)
    def _():
        rim_q[...] = jnp.zeros_like(rim_q)
        rim_k[...] = jnp.zeros_like(rim_k)
        rim_v[...] = jnp.zeros_like(rim_v)
        kv_before[...] = jnp.zeros_like(kv_before)
        state_in[...] = jnp.zeros_like(state_in)

    def arrived(copy):
        @pl.when(index > 0)
        def _():
            copy.wait_recv()

    first = index * rows
    offsets = [jnp.int32(0)]
    for d in range(docs - 1):
        offsets.append(offsets[-1] + doc_ref[d])

    def segments(position):
        total = jnp.zeros(position.shape, jnp.int32)
        for offset in offsets:
            total = total + jnp.where(position >= offset, 1, 0)
        return total

    square = (rows, rows)
    row_id = lax.broadcasted_iota(jnp.int32, square, 0)
    col_id = lax.broadcasted_iota(jnp.int32, square, 1)
    row_seg = segments(row_id + first)
    col_seg = segments(col_id + first)
    before_seg = segments(col_id + (first - rows))
    visible = (row_id >= col_id) & (row_seg == col_seg)
    visible_before = row_seg == before_seg
    strict = (row_id > col_id).astype(F32)
    carry_mask = row_seg == segments(jnp.zeros(square, jnp.int32) + (first - 1))
    same = [None] + [
        jnp.where(row_seg == segments(row_id + (first - s)), 1.0, 0.0) for s in (1, 2, 3)
    ]

    packed[...] = jnp.zeros_like(packed)
    packed[:, 0:heads] = log_decay[...]
    packed[:, heads : 2 * heads] = jax.nn.sigmoid(beta_logit[...])
    rates = packed[...]
    part_a = rates.astype(BF)
    rest = rates - part_a.astype(F32)
    part_b = rest.astype(BF)
    part_c = (rest - part_b.astype(F32)).astype(BF)
    tri = jnp.where(row_id >= col_id, 1.0, 0.0).astype(BF)
    summed = mm(
        jnp.concatenate([tri, tri, tri], axis=1), jnp.concatenate([part_a, part_b, part_c], axis=0)
    )
    columns = jnp.where(col_id < heads, summed, rates)
    flipped = columns.T
    carried = jnp.where(carry_mask & (col_id < heads), jnp.exp(jnp.minimum(columns, 0.0)), 0.0)

    eye = (row_id == col_id).astype(F32)

    def conv(values, spread, rim_ref, taps, at):
        width = pl.ds(at * LANES, LANES)
        spread[0:8, width] = rim_ref[rim - 8 : rim, width].astype(F32)
        spread[8 : 8 + rows, width] = values[:, width].astype(F32)
        total = spread[8 : 8 + rows, width] * taps[3:4, width].astype(F32)
        for s in (1, 2, 3):
            total = total + spread[8 - s : 8 - s + rows, width] * taps[
                3 - s : 4 - s, width
            ].astype(F32) * same[s]
        return total / (1.0 + jnp.exp(-total))

    def unit(x):
        return x * lax.rsqrt(jnp.sum(x * x, axis=1, keepdims=True) + 1e-06)

    for copy in early[:3]:
        arrived(copy)

    for g in range(GROUPS):
        members = range(g * per_group, (g + 1) * per_group)
        key_heads = range(g * per_group // shared, (g + 1) * per_group // shared)
        keys, query, scaled_keys, products = {}, {}, {}, {}
        for p in key_heads:
            keys[p] = unit(conv(lin_k, spread_k, rim_k, conv_k, p))
            query[p] = unit(conv(lin_q, spread_q, rim_q, conv_q, p)) * DK ** (-0.5)
        for p in key_heads:
            key_high, key_low = halves(keys[p])
            products[p] = mm(
                lhs3(jnp.concatenate([query[p], keys[p]], axis=0)),
                jnp.concatenate([key_high, key_high, key_low], axis=1),
                transposed=True,
            )
            scaled_keys[p] = keys[p].T
        lower, attend, weigh, right = {}, {}, {}, {}
        for h in members:
            p = h // shared
            gap = columns[:, h : h + 1] - flipped[h : h + 1, :]
            decay = jnp.exp(jnp.where(visible, gap, NEGATIVE)) * flipped[heads + h : heads + h + 1, :]
            attend[h] = lhs3(decay * products[p][:rows])
            lower[h] = decay * strict * products[p][rows:]
            weigh[h] = lhs3(scaled_keys[p] * decay[rows - 1 : rows, :])
            right[h] = jnp.concatenate(
                [conv(lin_v, spread_v, rim_v, conv_v, h), carried[:, h : h + 1] * keys[p]], axis=1
            )
        inverse = {}
        base = 8
        near = (row_id // base) == (col_id // base)
        power = {h: jnp.where(near, -lower[h], 0.0).astype(BF) for h in members}
        whole = {h: power[h].astype(F32) for h in members}
        power = {h: mm(power[h], power[h]).astype(BF) for h in members}
        for h in members:
            both = mm(jnp.concatenate([power[h], whole[h].astype(BF)], axis=0), power[h])
            whole[h] = whole[h] + power[h].astype(F32) + both[rows:]
            power[h] = both[:rows].astype(BF)
        for h in members:
            whole[h] = whole[h] + power[h].astype(F32) + mm(whole[h].astype(BF), power[h])
            inverse[h] = eye + whole[h]
        size = base
        while size < rows:
            joint = ((row_id // (2 * size)) == (col_id // (2 * size))) & (
                (row_id // size) != (col_id // size)
            )
            short = {h: inverse[h].astype(BF) for h in members}
            middle = {
                h: mm(short[h], jnp.where(joint, lower[h], 0.0).astype(BF)).astype(BF)
                for h in members
            }
            for h in members:
                inverse[h] = inverse[h] - mm(middle[h], short[h])
            size *= 2
        corrector = {h: (inverse[h] - eye).astype(BF) for h in members}
        solved = {h: right[h] + mm(corrector[h], right[h].astype(BF)) for h in members}
        residual = {
            h: right[h] - solved[h] - mm(lhs3(lower[h]), rhs3(solved[h])) for h in members
        }
        for h in members:
            solved[h] = solved[h] + residual[h] + mm(corrector[h], residual[h].astype(BF))
        stacked = {h: rhs3(solved[h]) for h in members}
        for h in members:
            state_out[h] = mm(weigh[h], stacked[h][:, :DV]).astype(BF)

        @pl.when(index < count - 1)
        def _(g=g):
            states[g].start()

        for h in members:
            mixed = mm(attend[h], stacked[h])
            local_out[h] = mixed[:, :DV]
            high, low = halves(carried[:, h : h + 1] * query[h // shared] - mixed[:, DV:])
            reach_out[h] = jnp.concatenate([high, low], axis=1)

    arrived(early[3])
    score_scale = AD ** (-0.5)
    allowed = jnp.concatenate([visible_before, visible], axis=1)
    all_keys = jnp.concatenate([kv_before[:, 0:AD], kv_own[:, 0:AD]], axis=0)
    all_values = jnp.concatenate([kv_before[:, AD:], kv_own[:, AD:]], axis=0)
    for a in range(attn_query.shape[1] // AD):
        width = pl.ds(a * AD, AD)
        scores = mm(attn_query[:, width], all_keys, transposed=True) * score_scale
        masked = jnp.where(allowed, scores, NEGATIVE)
        top = jnp.max(masked, axis=1, keepdims=True)
        weights = jnp.where(allowed, jnp.exp(masked - top), 0.0)
        total = jnp.sum(weights, axis=1, keepdims=True)
        mixture = mm(weights.astype(BF), all_values)
        gate = attn_gate[:, width].astype(F32)
        attn_out[:, width] = (mixture / total / (1.0 + jnp.exp(-gate))).astype(BF)

    for g in range(GROUPS):
        arrived(states[g])
        for h in range(g * per_group, (g + 1) * per_group):
            width = pl.ds(h * DV, DV)
            state = state_in[h]
            value = local_out[h] + mm(reach_out[h], jnp.concatenate([state, state], axis=0))
            scale = lax.rsqrt(jnp.mean(value * value, axis=1, keepdims=True) + 1e-06)
            gate = lin_z[:, width].astype(F32)
            delta_out[:, width] = (value * scale * (gate / (1.0 + jnp.exp(-gate)))).astype(BF)

    @pl.when(index < count - 1)
    def _():
        for copy in early + states:
            copy.wait_send()


def fused(
    lin_q,
    lin_k,
    lin_v,
    conv_q,
    conv_k,
    conv_v,
    lin_z,
    beta_logit,
    log_decay,
    attn_query,
    attn_gate,
    attn_kv,
    doc_lengths,
):
    rows = lin_q.shape[0]
    heads = lin_v.shape[1] // DV
    aq_local = attn_query.shape[1] // AD
    kv_head = lax.axis_index("head") * aq_local // (AQ // KVH)
    own_pair = lax.dynamic_index_in_dim(attn_kv, kv_head, axis=2, keepdims=False)
    own_pair = own_pair.reshape(rows, 2 * AD)
    vmem = pl.BlockSpec(memory_space=pltpu.VMEM)
    rim = 16
    copies = 4 + GROUPS
    return pl.pallas_call(
        functools.partial(fused_kernel, lax.axis_size("seq")),
        out_shape=(
            jax.ShapeDtypeStruct(lin_z.shape, BF),
            jax.ShapeDtypeStruct(attn_query.shape, BF),
        ),
        in_specs=[pl.BlockSpec(memory_space=pltpu.SMEM)] + [vmem] * 12,
        out_specs=(vmem, vmem),
        scratch_shapes=[
            pltpu.VMEM((rim, lin_q.shape[1]), BF),
            pltpu.VMEM((rim, lin_k.shape[1]), BF),
            pltpu.VMEM((rim, lin_v.shape[1]), BF),
            pltpu.VMEM(own_pair.shape, BF),
            pltpu.VMEM((heads, DK, DV), BF),
            pltpu.VMEM((heads, DK, DV), BF),
            pltpu.VMEM((rows + 8, lin_q.shape[1]), F32),
            pltpu.VMEM((rows + 8, lin_k.shape[1]), F32),
            pltpu.VMEM((rows + 8, lin_v.shape[1]), F32),
            pltpu.VMEM((rows, LANES), F32),
            pltpu.VMEM((heads, rows, DV), F32),
            pltpu.VMEM((heads, rows, 2 * DK), BF),
            pltpu.SemaphoreType.DMA((copies,)),
            pltpu.SemaphoreType.DMA((copies,)),
        ],
        compiler_params=pltpu.CompilerParams(
            collective_id=0, has_side_effects=True, vmem_limit_bytes=48 * 1024 * 1024
        ),
    )(
        doc_lengths,
        lin_q,
        lin_k,
        lin_v,
        conv_q,
        conv_k,
        conv_v,
        lin_z,
        beta_logit,
        log_decay,
        attn_query,
        attn_gate,
        own_pair,
    )


def solution(mesh):
    near = mesh.shape["seq"] == 4
    return jax.shard_map(
        fused if near else shards,
        mesh=mesh,
        in_specs=(
            P(("grp", "seq"), "head"),
            P(("grp", "seq"), "head"),
            P(("grp", "seq"), "head"),
            P(None, "head"),
            P(None, "head"),
            P(None, "head"),
            P(("grp", "seq"), "head"),
            P(("grp", "seq"), "head"),
            P(("grp", "seq"), "head"),
            P(("grp", "seq"), "head"),
            P(("grp", "seq"), "head"),
            P(("grp", "seq"), None, None, None),
            P("grp"),
        ),
        out_specs=(P(("grp", "seq"), "head"), P(("grp", "seq"), "head")),
        check_vma=False,
    )
```

```python
import functools

import jax
import jax.numpy as jnp
from jax import lax
from jax.experimental import pallas as pl
from jax.experimental.pallas import tpu as pltpu
from jax.sharding import PartitionSpec as P

DK = 128
DV = 128
QKH = 16
VALUE_HEADS = 32
AQ = 16
KVH = 2
AD = 256
BLOCK = 64


EXACT_PRECISION = lax.Precision.HIGHEST
NEGATIVE = -1e30


def passed_along(value, axis, steps):
    count = lax.axis_size(axis)
    initial, last = (max(0, -steps), min(count, count - steps))
    return lax.ppermute(value, axis, [(source, source + steps) for source in range(initial, last)])


def prefix_2(value, axis, combine, identity):
    length, index = (lax.axis_size(axis), lax.axis_index(axis))
    everything = jax.tree.map(
        lambda part, kind: lax.all_gather(part.astype(kind), axis),
        value,
        (jnp.bfloat16, jnp.bfloat16),
    )
    start = jax.tree.map(
        lambda part, zero: jnp.broadcast_to(jnp.asarray(zero, part.dtype), part.shape),
        value,
        identity,
    )

    def step(k, before):
        reached = k < index
        new = combine(
            before, jax.tree.map(lambda part, own: part[k].astype(own.dtype), everything, value)
        )
        return jax.tree.map(lambda a, b: jnp.where(reached, a, b), new, before)

    return lax.fori_loop(0, length, step, start)


def segment_ids(positions, doc_lengths):
    offsets = jnp.cumsum(doc_lengths) - doc_lengths
    return jnp.sum((offsets[None, :] <= positions[:, None]).astype(jnp.int32), axis=1)


def start_flags(positions, doc_lengths):
    offsets = jnp.cumsum(doc_lengths) - doc_lengths
    return jnp.any(offsets[None, :] == positions[:, None], axis=1)


def causal_conv(values, margin, weights, positions, segment, doc_lengths):
    row_count = values.shape[0]
    tap_count = weights.shape[0]
    extended = jnp.concatenate([margin, values], axis=0).astype(jnp.float32)
    conv_sum = jnp.zeros(values.shape, jnp.float32)
    for tap_index in range(tap_count):
        source = positions - (tap_count - 1) + tap_index
        inside = (segment_ids(source, doc_lengths) == segment).astype(jnp.float32)
        conv_sum = (
            conv_sum
            + extended[tap_index : tap_index + row_count]
            * weights[tap_index].astype(jnp.float32)[None, :]
            * inside[:, None]
        )
    return jax.nn.silu(conv_sum)


def unit_heads(values, head_size):
    shaped = values.reshape(values.shape[0], -1, head_size)
    return shaped * lax.rsqrt(jnp.sum(shaped * shaped, axis=-1, keepdims=True) + 1e-06)


def compose(first_pair, second_pair):
    joined_map = jnp.einsum(
        "hij,hjk->hik", second_pair[0], first_pair[0], precision=EXACT_PRECISION
    )
    joined_shift = (
        jnp.einsum("hij,hjk->hik", second_pair[0], first_pair[1], precision=EXACT_PRECISION)
        + second_pair[1]
    )
    return (joined_map, joined_shift)


def unit_lower_inverse(lower_part, block_len):
    identity = jnp.eye(block_len, dtype=jnp.float32)
    power = -lower_part
    inverse = identity + power
    for _ in range(max(block_len - 1, 1).bit_length() - 1):
        power = jnp.einsum("nhij,nhjk->nhik", power, power, precision=EXACT_PRECISION)
        inverse = jnp.einsum(
            "nhij,nhjk->nhik", inverse, identity + power, precision=EXACT_PRECISION
        )
    return inverse


def delta_blocks(queries, keys_unit, values, beta_gate, log_rates, segment, starts):
    row_count, head_count, key_size = keys_unit.shape
    value_size = values.shape[2]
    block_len = BLOCK
    block_count = row_count // block_len

    def to_blocks(array):
        return jnp.swapaxes(array.reshape((block_count, block_len) + array.shape[1:]), 1, 2)

    query_blk = to_blocks(queries)
    key_blk = to_blocks(keys_unit)
    value_blk = to_blocks(values)
    beta_blk = to_blocks(beta_gate)
    cumulative = jnp.cumsum(to_blocks(log_rates), axis=-1)
    segment_blk = segment.reshape(block_count, block_len)
    fresh_count = jnp.cumsum(starts.reshape(block_count, block_len).astype(jnp.int32), axis=-1)
    later_row = lax.broadcasted_iota(jnp.int32, (block_len, block_len), 0)
    earlier_col = lax.broadcasted_iota(jnp.int32, (block_len, block_len), 1)
    visible = (later_row >= earlier_col)[None] & (
        segment_blk[:, :, None] == segment_blk[:, None, :]
    )
    visible = visible[:, None]
    spread = cumulative[..., :, None] - cumulative[..., None, :]
    decay_mat = jnp.where(visible, jnp.exp(jnp.where(visible, spread, 0.0)), 0.0)
    carried = jnp.where((fresh_count == 0)[:, None, :], jnp.exp(cumulative), 0.0)
    key_key = jnp.einsum("nhik,nhjk->nhij", key_blk, key_blk, precision=EXACT_PRECISION)
    strict = (later_row > earlier_col).astype(jnp.float32)
    lower_part = decay_mat * strict * key_key * beta_blk[..., None, :]
    inverse = unit_lower_inverse(lower_part, block_len)
    right_side = jnp.concatenate([value_blk, carried[..., None] * key_blk], axis=-1)
    solved = jnp.einsum("nhij,nhjc->nhic", inverse, right_side, precision=EXACT_PRECISION)
    moved_values = solved[..., :value_size]
    moved_keys = solved[..., value_size:]
    query_key = jnp.einsum("nhik,nhjk->nhij", query_blk, key_blk, precision=EXACT_PRECISION)
    attend = decay_mat * query_key * beta_blk[..., None, :]
    out_zero = jnp.einsum("nhij,nhjv->nhiv", attend, moved_values, precision=EXACT_PRECISION)
    reach_part = carried[..., None] * query_blk - jnp.einsum(
        "nhij,nhjk->nhik", attend, moved_keys, precision=EXACT_PRECISION
    )
    weighted = (beta_blk * decay_mat[..., block_len - 1, :])[..., None] * key_blk
    block_map = carried[..., block_len - 1][..., None, None] * jnp.eye(
        key_size, dtype=jnp.float32
    ) - jnp.einsum("nhjk,nhjl->nhkl", weighted, moved_keys, precision=EXACT_PRECISION)
    block_shift = jnp.einsum("nhjk,nhjv->nhkv", weighted, moved_values, precision=EXACT_PRECISION)

    def advance(prefix, current):
        return (compose(prefix, current), prefix)

    eye_heads = jnp.broadcast_to(
        jnp.eye(key_size, dtype=jnp.float32), (head_count, key_size, key_size)
    )
    zero_heads = jnp.zeros((head_count, key_size, value_size), jnp.float32)
    device_pair, prefixes = lax.scan(advance, (eye_heads, zero_heads), (block_map, block_shift))
    baseline_output = out_zero + jnp.einsum(
        "nhik,nhkv->nhiv", reach_part, prefixes[1], precision=EXACT_PRECISION
    )
    complete_reach = jnp.einsum(
        "nhik,nhkl->nhil", reach_part, prefixes[0], precision=EXACT_PRECISION
    )
    return (device_pair, baseline_output, complete_reach, eye_heads, zero_heads)


def shards(
    lin_q,
    lin_k,
    lin_v,
    conv_q,
    conv_k,
    conv_v,
    lin_z,
    beta_logit,
    log_decay,
    attn_query,
    attn_gate,
    attn_kv,
    doc_lengths,
):
    row_count = lin_q.shape[0]
    seq_index = lax.axis_index("seq")
    positions = seq_index * row_count + jnp.arange(row_count, dtype=jnp.int32)
    segment = segment_ids(positions, doc_lengths)
    starts = start_flags(positions, doc_lengths)
    rim_from = row_count - conv_q.shape[0] + 1
    rim_q, rim_k, rim_v = passed_along(
        (lin_q[rim_from:], lin_k[rim_from:], lin_v[rim_from:]), "seq", 1
    )
    queries = unit_heads(
        causal_conv(lin_q, rim_q, conv_q, positions, segment, doc_lengths), DK
    ) * DK ** (-0.5)
    keys_unit = unit_heads(causal_conv(lin_k, rim_k, conv_k, positions, segment, doc_lengths), DK)
    values = causal_conv(lin_v, rim_v, conv_v, positions, segment, doc_lengths).reshape(
        row_count, -1, DV
    )
    head_count = values.shape[1]
    queries = jnp.repeat(queries, VALUE_HEADS // QKH, axis=1)
    keys_unit = jnp.repeat(keys_unit, VALUE_HEADS // QKH, axis=1)
    beta_gate = jax.nn.sigmoid(beta_logit)
    device_pair, baseline_output, complete_reach, eye_heads, zero_heads = delta_blocks(
        queries, keys_unit, values, beta_gate, log_decay, segment, starts
    )
    arriving_input = prefix_2(
        (device_pair[0], device_pair[1]), "seq", compose, (eye_heads, zero_heads)
    )
    delta_output = baseline_output + jnp.einsum(
        "dpjt,ptw->dpjw", complete_reach, arriving_input[1], precision=EXACT_PRECISION
    )
    delta_output = jnp.swapaxes(delta_output, 1, 2).reshape(row_count, head_count, DV)
    inverse_rms = lax.rsqrt(jnp.mean(delta_output * delta_output, axis=-1, keepdims=True) + 1e-06)
    gate_z = jax.nn.silu(lin_z.astype(jnp.float32).reshape(row_count, head_count, DV))
    delta_out = (
        (delta_output * inverse_rms * gate_z)
        .astype(jnp.bfloat16)
        .reshape(row_count, head_count * DV)
    )
    aq_local = attn_query.shape[1] // AD
    query_heads = attn_query.reshape(row_count, aq_local, AD)
    kv_head = lax.axis_index("head") * aq_local // (AQ // KVH)
    own_pair = lax.dynamic_index_in_dim(attn_kv, kv_head, axis=2, keepdims=False)
    score_scale = AD ** (-0.5)

    def absorb(running, kv_piece, first_row):
        row_top, row_total, accum = running
        piece_rows = kv_piece.shape[0]
        key_pos = first_row + jnp.arange(piece_rows, dtype=jnp.int32)
        key_seg = segment_ids(key_pos, doc_lengths)
        allowed = (
            (key_pos[None, :] <= positions[:, None])
            & (key_seg[None, :] == segment[:, None])
            & (key_pos[None, :] >= 0)
        )
        scores = (
            jnp.einsum(
                "qhd,kd->hqk", query_heads, kv_piece[:, 0], preferred_element_type=jnp.float32
            )
            * score_scale
        )
        masked = jnp.where(allowed[None], scores, NEGATIVE)
        new_top = jnp.maximum(row_top, jnp.max(masked, axis=-1))
        weights_f = jnp.where(allowed[None], jnp.exp(masked - new_top[..., None]), 0.0)
        rescale = jnp.exp(row_top - new_top)
        row_total = row_total * rescale + jnp.sum(weights_f, axis=-1)
        accum = accum * rescale[..., None] + jnp.einsum(
            "hqk,kd->hqd",
            weights_f.astype(jnp.bfloat16),
            kv_piece[:, 1],
            preferred_element_type=jnp.float32,
        )
        return (new_top, row_total, accum)

    start_state = (
        jnp.full((aq_local, row_count), NEGATIVE, jnp.float32),
        jnp.zeros((aq_local, row_count), jnp.float32),
        jnp.zeros((aq_local, row_count, AD), jnp.float32),
    )
    running = absorb(start_state, own_pair, seq_index * row_count)

    def hop(hop_step, loop_state):
        loop_running, kv_piece = loop_state
        kv_piece = passed_along(kv_piece, "seq", 1)
        loop_running = absorb(loop_running, kv_piece, (seq_index - hop_step - 1) * row_count)
        return (loop_running, kv_piece)

    running, _ = lax.fori_loop(0, lax.axis_size("seq") // 4, hop, (running, own_pair))
    row_top, row_total, accum = running
    attended = jnp.swapaxes(accum / row_total[..., None], 0, 1).reshape(row_count, aq_local * AD)
    attn_out = (attended * jax.nn.sigmoid(attn_gate.astype(jnp.float32))).astype(jnp.bfloat16)
    return (delta_out, attn_out)


BF = jnp.bfloat16
F32 = jnp.float32
LANES = 128
GROUPS = 2


def mm(a, b, transposed=False):
    contract = ((1,), (1,)) if transposed else ((1,), (0,))
    return lax.dot_general(a, b, (contract, ((), ())), preferred_element_type=F32)


def halves(x):
    high = x.astype(BF)
    return high, (x - high.astype(F32)).astype(BF)


def block_diagonal(wide):
    zero = jnp.zeros((wide.shape[0], LANES), wide.dtype)
    return jnp.concatenate(
        [
            jnp.concatenate([wide[:, :LANES], zero], axis=1),
            jnp.concatenate([zero, wide[:, LANES:]], axis=1),
        ],
        axis=0,
    )


def twice(x):
    return jnp.concatenate([x, x], axis=1)


def fused_kernel(
    count,
    doc_ref,
    kv_own,
    lin_q_hbm,
    lin_k_hbm,
    lin_v_hbm,
    conv_q_hbm,
    conv_k_hbm,
    conv_v_hbm,
    lin_z_hbm,
    beta_hbm,
    decay_hbm,
    attn_query_hbm,
    attn_gate_hbm,
    delta_out,
    attn_out,
    lin_q,
    lin_k,
    lin_v,
    conv_q,
    conv_k,
    conv_v,
    lin_z,
    beta_logit,
    log_decay,
    attn_query,
    attn_gate,
    rim_q,
    rim_k,
    rim_v,
    kv_before,
    state_out,
    state_in,
    spread_q,
    spread_k,
    spread_v,
    local_out,
    reach_out,
    gates,
    send_sem,
    recv_sem,
    load_sem,
):
    rows = lin_q.shape[0]
    heads = lin_v.shape[1] // DV
    pairs = range(lin_k.shape[1] // DK)
    docs = doc_ref.shape[0]
    rim = rim_q.shape[0]
    index = lax.axis_index("seq")
    barrier = pltpu.get_barrier_semaphore()

    @pl.when(index > 0)
    def _():
        pl.semaphore_signal(
            barrier, inc=1, device_id={"seq": index - 1}, device_id_type=pl.DeviceIdType.MESH
        )

    loads = {}
    order = [
        ("decay", decay_hbm, log_decay),
        ("beta", beta_hbm, beta_logit),
        ("taps_k", conv_k_hbm, conv_k),
        ("k", lin_k_hbm, lin_k),
        ("taps_v", conv_v_hbm, conv_v),
        ("v", lin_v_hbm, lin_v),
        ("taps_q", conv_q_hbm, conv_q),
        ("q", lin_q_hbm, lin_q),
        ("query", attn_query_hbm, attn_query),
        ("gate", attn_gate_hbm, attn_gate),
        ("z", lin_z_hbm, lin_z),
    ]
    for slot, (name, source, target) in enumerate(order):
        loads[name] = pltpu.make_async_copy(source, target, load_sem.at[slot])
        loads[name].start()

    def transfer(source, target, slot):
        return pltpu.make_async_remote_copy(
            src_ref=source,
            dst_ref=target,
            send_sem=send_sem.at[slot],
            recv_sem=recv_sem.at[slot],
            device_id={"seq": index + 1},
            device_id_type=pl.DeviceIdType.MESH,
        )

    tail = pl.ds(rows - rim, rim)
    early = [
        transfer(lin_k_hbm.at[tail, :], rim_k, 0),
        transfer(lin_v_hbm.at[tail, :], rim_v, 1),
        transfer(lin_q_hbm.at[tail, :], rim_q, 2),
        transfer(kv_own, kv_before, 3),
    ]
    states = transfer(state_out, state_in, 4)

    @pl.when(index < count - 1)
    def _():
        pl.semaphore_wait(barrier, 1)
        for copy in early:
            copy.start()

    @pl.when(index == 0)
    def _():
        rim_q[...] = jnp.zeros_like(rim_q)
        rim_k[...] = jnp.zeros_like(rim_k)
        rim_v[...] = jnp.zeros_like(rim_v)
        kv_before[...] = jnp.zeros_like(kv_before)
        state_in[...] = jnp.zeros_like(state_in)

    def arrived(*copies):
        @pl.when(index > 0)
        def _():
            for copy in copies:
                copy.wait_recv()

    first = index * rows
    offsets = [jnp.int32(0)]
    for d in range(docs - 1):
        offsets.append(offsets[-1] + doc_ref[d])

    def segments(position):
        total = jnp.zeros(position.shape, jnp.int32)
        for offset in offsets:
            total = total + jnp.where(position >= offset, 1, 0)
        return total

    square = (rows, rows)
    row_id = lax.broadcasted_iota(jnp.int32, square, 0)
    col_id = lax.broadcasted_iota(jnp.int32, square, 1)
    row_seg = segments(row_id + first)
    col_seg = segments(col_id + first)
    before_seg = segments(col_id + (first - rows))
    visible = (row_id >= col_id) & (row_seg == col_seg)
    visible_before = row_seg == before_seg
    strict = row_id > col_id
    same = [None] + [
        jnp.where(row_seg == segments(row_id + (first - s)), 1.0, 0.0) for s in (1, 2, 3)
    ]
    short_seg = segments(lax.broadcasted_iota(jnp.int32, (heads, rows), 1) + first)
    last_seg = segments(jnp.full((heads, rows), rows - 1, jnp.int32) + first)
    prior_seg = segments(jnp.zeros((heads, rows), jnp.int32) + (first - 1))

    loads["decay"].wait()
    loads["beta"].wait()
    rates = log_decay[...]
    beta = jax.nn.sigmoid(beta_logit[...])
    part_a = rates.astype(BF)
    rest = rates - part_a.astype(F32)
    part_b = rest.astype(BF)
    part_c = (rest - part_b.astype(F32)).astype(BF)
    upper = jnp.where(row_id <= col_id, 1.0, 0.0).astype(BF)
    summed = mm(part_a, upper) + mm(part_b, upper) + mm(part_c, upper)
    carried_row = jnp.where(short_seg == prior_seg, jnp.exp(summed), 0.0)
    ending = jnp.where(
        short_seg == last_seg, jnp.exp(summed[:, rows - 1 : rows] - summed), 0.0
    )
    columns = jnp.concatenate(
        [
            summed,
            carried_row,
            beta * ending,
            jnp.zeros((rows - 3 * heads, rows), F32),
        ],
        axis=0,
    ).T
    carried = [columns[:, heads + h : heads + h + 1] for h in range(heads)]
    closing = [columns[:, 2 * heads + h : 2 * heads + h + 1] for h in range(heads)]

    def decays(h):
        gap = columns[:, h : h + 1] - summed[h : h + 1, :]
        return jnp.exp(jnp.where(visible, gap, NEGATIVE)) * beta[h : h + 1, :]

    def conv(values, spread, rim_ref, taps, at):
        width = pl.ds(at * LANES, LANES)
        spread[0:8, width] = rim_ref[rim - 8 : rim, width].astype(F32)
        spread[8 : 8 + rows, width] = values[:, width].astype(F32)
        total = spread[8 : 8 + rows, width] * taps[3:4, width].astype(F32)
        for s in (1, 2, 3):
            total = total + spread[8 - s : 8 - s + rows, width] * taps[
                3 - s : 4 - s, width
            ].astype(F32) * same[s]
        return total / (1.0 + jnp.exp(-total))

    def unit(x):
        return x * lax.rsqrt(jnp.sum(x * x, axis=1, keepdims=True) + 1e-06)

    for name in ("taps_k", "k", "taps_v", "v"):
        loads[name].wait()
    arrived(*early[:3])

    keys = {p: unit(conv(lin_k, spread_k, rim_k, conv_k, p)) for p in pairs}
    key_high, key_low, key_right = {}, {}, {}
    for p in pairs:
        key_high[p], key_low[p] = halves(keys[p])
        key_right[p] = jnp.concatenate([key_high[p], key_high[p], key_low[p]], axis=1)
    lower, decay = {}, {}
    for p in pairs:
        product = mm(
            jnp.concatenate([key_high[p], key_low[p], key_high[p]], axis=1),
            key_right[p],
            transposed=True,
        )
        product = jnp.where(strict, product, 0.0)
        for h in (2 * p, 2 * p + 1):
            decay[h] = decays(h)
        lower[p] = jnp.concatenate(
            [decay[2 * p] * product, decay[2 * p + 1] * product], axis=1
        )
    base = 8
    near = twice((row_id // base) == (col_id // base))
    eye = twice(jnp.where(row_id == col_id, 1.0, 0.0))
    power = {p: jnp.where(near, -lower[p], 0.0).astype(BF) for p in pairs}
    whole = {p: power[p].astype(F32) for p in pairs}
    power = {p: mm(power[p], block_diagonal(power[p])).astype(BF) for p in pairs}
    for p in pairs:
        both = mm(
            jnp.concatenate([power[p], whole[p].astype(BF)], axis=0), block_diagonal(power[p])
        )
        whole[p] = whole[p] + power[p].astype(F32) + both[rows:]
        power[p] = both[:rows].astype(BF)
    inverse = {
        p: eye
        + whole[p]
        + power[p].astype(F32)
        + mm(whole[p].astype(BF), block_diagonal(power[p]))
        for p in pairs
    }
    size = base
    while size < rows:
        joint = twice(
            ((row_id // (2 * size)) == (col_id // (2 * size)))
            & ((row_id // size) != (col_id // size))
        )
        short = {p: inverse[p].astype(BF) for p in pairs}
        middle = {
            p: mm(short[p], block_diagonal(jnp.where(joint, lower[p], 0.0).astype(BF))).astype(BF)
            for p in pairs
        }
        for p in pairs:
            inverse[p] = inverse[p] - mm(middle[p], block_diagonal(short[p]))
        size *= 2
    corrector, solved, refined, right, split_lower = {}, {}, {}, {}, {}
    for p in pairs:
        corrector_pair = (inverse[p] - eye).astype(BF)
        high, low = halves(lower[p])
        for half in range(2):
            h = 2 * p + half
            lanes = slice(half * LANES, (half + 1) * LANES)
            corrector[h] = corrector_pair[:, lanes]
            split_lower[h] = jnp.concatenate([high[:, lanes], low[:, lanes]], axis=1)
            right[h] = jnp.concatenate(
                [conv(lin_v, spread_v, rim_v, conv_v, h), carried[h] * keys[p]], axis=1
            )
    for h in range(heads):
        solved[h] = (right[h] + mm(corrector[h], right[h].astype(BF))).astype(BF)
    for h in range(heads):
        right[h] = (
            right[h]
            - solved[h].astype(F32)
            - mm(split_lower[h], jnp.concatenate([solved[h], solved[h]], axis=0))
        )
    for h in range(heads):
        refined[h] = (right[h] + mm(corrector[h], right[h].astype(BF))).astype(BF)
    for p in pairs:
        parts = [
            closing[h] * (solved[h][:, :DV].astype(F32) + refined[h][:, :DV].astype(F32))
            for h in (2 * p, 2 * p + 1)
        ]
        wide = jnp.concatenate(parts, axis=1).astype(BF)
        high, low = halves(keys[p].T)
        made = mm(
            jnp.concatenate([high, low], axis=1), jnp.concatenate([wide, wide], axis=0)
        ).astype(BF)
        state_out[2 * p] = made[:, :DV]
        state_out[2 * p + 1] = made[:, DV:]

    @pl.when(index < count - 1)
    def _():
        states.start()

    arrived(early[3])
    for name in ("taps_q", "q", "query", "gate", "z"):
        loads[name].wait()

    for p in pairs:
        query = unit(conv(lin_q, spread_q, rim_q, conv_q, p)) * DK ** (-0.5)
        high, low = halves(query)
        product = mm(jnp.concatenate([high, low, high], axis=1), key_right[p], transposed=True)
        for h in (2 * p, 2 * p + 1):
            high, low = halves(decay[h] * product)
            mixed = mm(
                jnp.concatenate([high, low], axis=1),
                jnp.concatenate([solved[h], solved[h]], axis=0),
            ) + mm(high, refined[h])
            local_out[h] = mixed[:, :DV]
            high, low = halves(carried[h] * query - mixed[:, DV:])
            reach_out[h] = jnp.concatenate([high, low], axis=1)

    score_scale = AD ** (-0.5)
    allowed = jnp.concatenate([visible_before, visible], axis=1)
    all_keys = jnp.concatenate([kv_before[:, 0:AD], kv_own[:, 0:AD]], axis=0)
    all_values = jnp.concatenate([kv_before[:, AD:], kv_own[:, AD:]], axis=0)
    for a in range(attn_query.shape[1] // AD):
        width = pl.ds(a * AD, AD)
        scores = mm(attn_query[:, width], all_keys, transposed=True) * score_scale
        masked = jnp.where(allowed, scores, NEGATIVE)
        top = jnp.max(masked, axis=1, keepdims=True)
        weights = jnp.where(allowed, jnp.exp(masked - top), 0.0)
        total = jnp.sum(weights, axis=1, keepdims=True)
        mixture = mm(weights.astype(BF), all_values)
        gate = attn_gate[:, width].astype(F32)
        attn_out[:, width] = (mixture * (1.0 / total) / (1.0 + jnp.exp(-gate))).astype(BF)
    for h in range(heads):
        gate = lin_z[:, pl.ds(h * DV, DV)].astype(F32)
        gates[h] = gate / (1.0 + jnp.exp(-gate))

    arrived(states)
    for h in range(heads):
        state = state_in[h]
        value = local_out[h] + mm(reach_out[h], jnp.concatenate([state, state], axis=0))
        scale = lax.rsqrt(jnp.mean(value * value, axis=1, keepdims=True) + 1e-06)
        delta_out[:, pl.ds(h * DV, DV)] = (value * scale * gates[h]).astype(BF)

    @pl.when(index < count - 1)
    def _():
        for copy in early + [states]:
            copy.wait_send()


def fused(
    lin_q,
    lin_k,
    lin_v,
    conv_q,
    conv_k,
    conv_v,
    lin_z,
    beta_logit,
    log_decay,
    attn_query,
    attn_gate,
    attn_kv,
    doc_lengths,
):
    rows = lin_q.shape[0]
    heads = lin_v.shape[1] // DV
    aq_local = attn_query.shape[1] // AD
    kv_head = lax.axis_index("head") * aq_local // (AQ // KVH)
    own_pair = lax.dynamic_index_in_dim(attn_kv, kv_head, axis=2, keepdims=False)
    own_pair = own_pair.reshape(rows, 2 * AD)
    streamed = (
        lin_q,
        lin_k,
        lin_v,
        conv_q,
        conv_k,
        conv_v,
        lin_z,
        beta_logit.T,
        log_decay.T,
        attn_query,
        attn_gate,
    )
    vmem = pl.BlockSpec(memory_space=pltpu.VMEM)
    rim = 16
    return pl.pallas_call(
        functools.partial(fused_kernel, lax.axis_size("seq")),
        out_shape=(
            jax.ShapeDtypeStruct(lin_z.shape, BF),
            jax.ShapeDtypeStruct(attn_query.shape, BF),
        ),
        in_specs=[pl.BlockSpec(memory_space=pltpu.SMEM), vmem]
        + [pl.BlockSpec(memory_space=pltpu.HBM)] * len(streamed),
        out_specs=(vmem, vmem),
        scratch_shapes=[pltpu.VMEM(x.shape, x.dtype) for x in streamed]
        + [
            pltpu.VMEM((rim, lin_q.shape[1]), BF),
            pltpu.VMEM((rim, lin_k.shape[1]), BF),
            pltpu.VMEM((rim, lin_v.shape[1]), BF),
            pltpu.VMEM(own_pair.shape, BF),
            pltpu.VMEM((heads, DK, DV), BF),
            pltpu.VMEM((heads, DK, DV), BF),
            pltpu.VMEM((rows + 8, lin_q.shape[1]), F32),
            pltpu.VMEM((rows + 8, lin_k.shape[1]), F32),
            pltpu.VMEM((rows + 8, lin_v.shape[1]), F32),
            pltpu.VMEM((heads, rows, DV), F32),
            pltpu.VMEM((heads, rows, 2 * DK), BF),
            pltpu.VMEM((heads, rows, DV), F32),
            pltpu.SemaphoreType.DMA((5,)),
            pltpu.SemaphoreType.DMA((5,)),
            pltpu.SemaphoreType.DMA((len(streamed),)),
        ],
        compiler_params=pltpu.CompilerParams(
            collective_id=0, has_side_effects=True, vmem_limit_bytes=48 * 1024 * 1024
        ),
    )(doc_lengths, own_pair, *streamed)


def solution(mesh):
    near = mesh.shape["seq"] == 4
    return jax.shard_map(
        fused if near else shards,
        mesh=mesh,
        in_specs=(
            P(("grp", "seq"), "head"),
            P(("grp", "seq"), "head"),
            P(("grp", "seq"), "head"),
            P(None, "head"),
            P(None, "head"),
            P(None, "head"),
            P(("grp", "seq"), "head"),
            P(("grp", "seq"), "head"),
            P(("grp", "seq"), "head"),
            P(("grp", "seq"), "head"),
            P(("grp", "seq"), "head"),
            P(("grp", "seq"), None, None, None),
            P("grp"),
        ),
        out_specs=(P(("grp", "seq"), "head"), P(("grp", "seq"), "head")),
        check_vma=False,
    )
```

```python
import functools

import jax
import jax.numpy as jnp
from jax import lax
from jax.experimental import pallas as pl
from jax.experimental.pallas import tpu as pltpu
from jax.sharding import PartitionSpec as P

DK = 128
DV = 128
QKH = 16
VALUE_HEADS = 32
AQ = 16
KVH = 2
AD = 256
BLOCK = 64


EXACT_PRECISION = lax.Precision.HIGHEST
NEGATIVE = -1e30


def passed_along(value, axis, steps):
    count = lax.axis_size(axis)
    initial, last = (max(0, -steps), min(count, count - steps))
    return lax.ppermute(value, axis, [(source, source + steps) for source in range(initial, last)])


def prefix_2(value, axis, combine, identity):
    length, index = (lax.axis_size(axis), lax.axis_index(axis))
    everything = jax.tree.map(
        lambda part, kind: lax.all_gather(part.astype(kind), axis),
        value,
        (jnp.bfloat16, jnp.bfloat16),
    )
    start = jax.tree.map(
        lambda part, zero: jnp.broadcast_to(jnp.asarray(zero, part.dtype), part.shape),
        value,
        identity,
    )

    def step(k, before):
        reached = k < index
        new = combine(
            before, jax.tree.map(lambda part, own: part[k].astype(own.dtype), everything, value)
        )
        return jax.tree.map(lambda a, b: jnp.where(reached, a, b), new, before)

    return lax.fori_loop(0, length, step, start)


def segment_ids(positions, doc_lengths):
    offsets = jnp.cumsum(doc_lengths) - doc_lengths
    return jnp.sum((offsets[None, :] <= positions[:, None]).astype(jnp.int32), axis=1)


def start_flags(positions, doc_lengths):
    offsets = jnp.cumsum(doc_lengths) - doc_lengths
    return jnp.any(offsets[None, :] == positions[:, None], axis=1)


def causal_conv(values, margin, weights, positions, segment, doc_lengths):
    row_count = values.shape[0]
    tap_count = weights.shape[0]
    extended = jnp.concatenate([margin, values], axis=0).astype(jnp.float32)
    conv_sum = jnp.zeros(values.shape, jnp.float32)
    for tap_index in range(tap_count):
        source = positions - (tap_count - 1) + tap_index
        inside = (segment_ids(source, doc_lengths) == segment).astype(jnp.float32)
        conv_sum = (
            conv_sum
            + extended[tap_index : tap_index + row_count]
            * weights[tap_index].astype(jnp.float32)[None, :]
            * inside[:, None]
        )
    return jax.nn.silu(conv_sum)


def unit_heads(values, head_size):
    shaped = values.reshape(values.shape[0], -1, head_size)
    return shaped * lax.rsqrt(jnp.sum(shaped * shaped, axis=-1, keepdims=True) + 1e-06)


def compose(first_pair, second_pair):
    joined_map = jnp.einsum(
        "hij,hjk->hik", second_pair[0], first_pair[0], precision=EXACT_PRECISION
    )
    joined_shift = (
        jnp.einsum("hij,hjk->hik", second_pair[0], first_pair[1], precision=EXACT_PRECISION)
        + second_pair[1]
    )
    return (joined_map, joined_shift)


def unit_lower_inverse(lower_part, block_len):
    identity = jnp.eye(block_len, dtype=jnp.float32)
    power = -lower_part
    inverse = identity + power
    for _ in range(max(block_len - 1, 1).bit_length() - 1):
        power = jnp.einsum("nhij,nhjk->nhik", power, power, precision=EXACT_PRECISION)
        inverse = jnp.einsum(
            "nhij,nhjk->nhik", inverse, identity + power, precision=EXACT_PRECISION
        )
    return inverse


def delta_blocks(queries, keys_unit, values, beta_gate, log_rates, segment, starts):
    row_count, head_count, key_size = keys_unit.shape
    value_size = values.shape[2]
    block_len = BLOCK
    block_count = row_count // block_len

    def to_blocks(array):
        return jnp.swapaxes(array.reshape((block_count, block_len) + array.shape[1:]), 1, 2)

    query_blk = to_blocks(queries)
    key_blk = to_blocks(keys_unit)
    value_blk = to_blocks(values)
    beta_blk = to_blocks(beta_gate)
    cumulative = jnp.cumsum(to_blocks(log_rates), axis=-1)
    segment_blk = segment.reshape(block_count, block_len)
    fresh_count = jnp.cumsum(starts.reshape(block_count, block_len).astype(jnp.int32), axis=-1)
    later_row = lax.broadcasted_iota(jnp.int32, (block_len, block_len), 0)
    earlier_col = lax.broadcasted_iota(jnp.int32, (block_len, block_len), 1)
    visible = (later_row >= earlier_col)[None] & (
        segment_blk[:, :, None] == segment_blk[:, None, :]
    )
    visible = visible[:, None]
    spread = cumulative[..., :, None] - cumulative[..., None, :]
    decay_mat = jnp.where(visible, jnp.exp(jnp.where(visible, spread, 0.0)), 0.0)
    carried = jnp.where((fresh_count == 0)[:, None, :], jnp.exp(cumulative), 0.0)
    key_key = jnp.einsum("nhik,nhjk->nhij", key_blk, key_blk, precision=EXACT_PRECISION)
    strict = (later_row > earlier_col).astype(jnp.float32)
    lower_part = decay_mat * strict * key_key * beta_blk[..., None, :]
    inverse = unit_lower_inverse(lower_part, block_len)
    right_side = jnp.concatenate([value_blk, carried[..., None] * key_blk], axis=-1)
    solved = jnp.einsum("nhij,nhjc->nhic", inverse, right_side, precision=EXACT_PRECISION)
    moved_values = solved[..., :value_size]
    moved_keys = solved[..., value_size:]
    query_key = jnp.einsum("nhik,nhjk->nhij", query_blk, key_blk, precision=EXACT_PRECISION)
    attend = decay_mat * query_key * beta_blk[..., None, :]
    out_zero = jnp.einsum("nhij,nhjv->nhiv", attend, moved_values, precision=EXACT_PRECISION)
    reach_part = carried[..., None] * query_blk - jnp.einsum(
        "nhij,nhjk->nhik", attend, moved_keys, precision=EXACT_PRECISION
    )
    weighted = (beta_blk * decay_mat[..., block_len - 1, :])[..., None] * key_blk
    block_map = carried[..., block_len - 1][..., None, None] * jnp.eye(
        key_size, dtype=jnp.float32
    ) - jnp.einsum("nhjk,nhjl->nhkl", weighted, moved_keys, precision=EXACT_PRECISION)
    block_shift = jnp.einsum("nhjk,nhjv->nhkv", weighted, moved_values, precision=EXACT_PRECISION)

    def advance(prefix, current):
        return (compose(prefix, current), prefix)

    eye_heads = jnp.broadcast_to(
        jnp.eye(key_size, dtype=jnp.float32), (head_count, key_size, key_size)
    )
    zero_heads = jnp.zeros((head_count, key_size, value_size), jnp.float32)
    device_pair, prefixes = lax.scan(advance, (eye_heads, zero_heads), (block_map, block_shift))
    baseline_output = out_zero + jnp.einsum(
        "nhik,nhkv->nhiv", reach_part, prefixes[1], precision=EXACT_PRECISION
    )
    complete_reach = jnp.einsum(
        "nhik,nhkl->nhil", reach_part, prefixes[0], precision=EXACT_PRECISION
    )
    return (device_pair, baseline_output, complete_reach, eye_heads, zero_heads)


def shards(
    lin_q,
    lin_k,
    lin_v,
    conv_q,
    conv_k,
    conv_v,
    lin_z,
    beta_logit,
    log_decay,
    attn_query,
    attn_gate,
    attn_kv,
    doc_lengths,
):
    row_count = lin_q.shape[0]
    seq_index = lax.axis_index("seq")
    positions = seq_index * row_count + jnp.arange(row_count, dtype=jnp.int32)
    segment = segment_ids(positions, doc_lengths)
    starts = start_flags(positions, doc_lengths)
    rim_from = row_count - conv_q.shape[0] + 1
    rim_q, rim_k, rim_v = passed_along(
        (lin_q[rim_from:], lin_k[rim_from:], lin_v[rim_from:]), "seq", 1
    )
    queries = unit_heads(
        causal_conv(lin_q, rim_q, conv_q, positions, segment, doc_lengths), DK
    ) * DK ** (-0.5)
    keys_unit = unit_heads(causal_conv(lin_k, rim_k, conv_k, positions, segment, doc_lengths), DK)
    values = causal_conv(lin_v, rim_v, conv_v, positions, segment, doc_lengths).reshape(
        row_count, -1, DV
    )
    head_count = values.shape[1]
    queries = jnp.repeat(queries, VALUE_HEADS // QKH, axis=1)
    keys_unit = jnp.repeat(keys_unit, VALUE_HEADS // QKH, axis=1)
    beta_gate = jax.nn.sigmoid(beta_logit)
    device_pair, baseline_output, complete_reach, eye_heads, zero_heads = delta_blocks(
        queries, keys_unit, values, beta_gate, log_decay, segment, starts
    )
    arriving_input = prefix_2(
        (device_pair[0], device_pair[1]), "seq", compose, (eye_heads, zero_heads)
    )
    delta_output = baseline_output + jnp.einsum(
        "dpjt,ptw->dpjw", complete_reach, arriving_input[1], precision=EXACT_PRECISION
    )
    delta_output = jnp.swapaxes(delta_output, 1, 2).reshape(row_count, head_count, DV)
    inverse_rms = lax.rsqrt(jnp.mean(delta_output * delta_output, axis=-1, keepdims=True) + 1e-06)
    gate_z = jax.nn.silu(lin_z.astype(jnp.float32).reshape(row_count, head_count, DV))
    delta_out = (
        (delta_output * inverse_rms * gate_z)
        .astype(jnp.bfloat16)
        .reshape(row_count, head_count * DV)
    )
    aq_local = attn_query.shape[1] // AD
    query_heads = attn_query.reshape(row_count, aq_local, AD)
    kv_head = lax.axis_index("head") * aq_local // (AQ // KVH)
    own_pair = lax.dynamic_index_in_dim(attn_kv, kv_head, axis=2, keepdims=False)
    score_scale = AD ** (-0.5)

    def absorb(running, kv_piece, first_row):
        row_top, row_total, accum = running
        piece_rows = kv_piece.shape[0]
        key_pos = first_row + jnp.arange(piece_rows, dtype=jnp.int32)
        key_seg = segment_ids(key_pos, doc_lengths)
        allowed = (
            (key_pos[None, :] <= positions[:, None])
            & (key_seg[None, :] == segment[:, None])
            & (key_pos[None, :] >= 0)
        )
        scores = (
            jnp.einsum(
                "qhd,kd->hqk", query_heads, kv_piece[:, 0], preferred_element_type=jnp.float32
            )
            * score_scale
        )
        masked = jnp.where(allowed[None], scores, NEGATIVE)
        new_top = jnp.maximum(row_top, jnp.max(masked, axis=-1))
        weights_f = jnp.where(allowed[None], jnp.exp(masked - new_top[..., None]), 0.0)
        rescale = jnp.exp(row_top - new_top)
        row_total = row_total * rescale + jnp.sum(weights_f, axis=-1)
        accum = accum * rescale[..., None] + jnp.einsum(
            "hqk,kd->hqd",
            weights_f.astype(jnp.bfloat16),
            kv_piece[:, 1],
            preferred_element_type=jnp.float32,
        )
        return (new_top, row_total, accum)

    start_state = (
        jnp.full((aq_local, row_count), NEGATIVE, jnp.float32),
        jnp.zeros((aq_local, row_count), jnp.float32),
        jnp.zeros((aq_local, row_count, AD), jnp.float32),
    )
    running = absorb(start_state, own_pair, seq_index * row_count)

    def hop(hop_step, loop_state):
        loop_running, kv_piece = loop_state
        kv_piece = passed_along(kv_piece, "seq", 1)
        loop_running = absorb(loop_running, kv_piece, (seq_index - hop_step - 1) * row_count)
        return (loop_running, kv_piece)

    running, _ = lax.fori_loop(0, lax.axis_size("seq") // 4, hop, (running, own_pair))
    row_top, row_total, accum = running
    attended = jnp.swapaxes(accum / row_total[..., None], 0, 1).reshape(row_count, aq_local * AD)
    attn_out = (attended * jax.nn.sigmoid(attn_gate.astype(jnp.float32))).astype(jnp.bfloat16)
    return (delta_out, attn_out)


BF = jnp.bfloat16
F32 = jnp.float32
LANES = 128
GROUPS = 2


def mm(a, b, transposed=False):
    contract = ((1,), (1,)) if transposed else ((1,), (0,))
    return lax.dot_general(a, b, (contract, ((), ())), preferred_element_type=F32)


def halves(x):
    high = x.astype(BF)
    return high, (x - high.astype(F32)).astype(BF)


def block_diagonal(wide):
    zero = jnp.zeros((wide.shape[0], LANES), wide.dtype)
    return jnp.concatenate(
        [
            jnp.concatenate([wide[:, :LANES], zero], axis=1),
            jnp.concatenate([zero, wide[:, LANES:]], axis=1),
        ],
        axis=0,
    )


def twice(x):
    return jnp.concatenate([x, x], axis=1)


def fused_kernel(
    count,
    doc_ref,
    kv_own,
    lin_q_hbm,
    lin_k_hbm,
    lin_v_hbm,
    conv_q_hbm,
    conv_k_hbm,
    conv_v_hbm,
    lin_z_hbm,
    beta_hbm,
    decay_hbm,
    attn_query_hbm,
    attn_gate_hbm,
    delta_out,
    attn_out,
    lin_q,
    lin_k,
    lin_v,
    conv_q,
    conv_k,
    conv_v,
    lin_z,
    beta_logit,
    log_decay,
    attn_query,
    attn_gate,
    rim_q,
    rim_k,
    rim_v,
    kv_before,
    state_out,
    state_in,
    spread_q,
    spread_k,
    spread_v,
    local_out,
    reach_out,
    gates,
    send_sem,
    recv_sem,
    load_sem,
):
    rows = lin_q.shape[0]
    heads = lin_v.shape[1] // DV
    pairs = range(lin_k.shape[1] // DK)
    docs = doc_ref.shape[0]
    rim = rim_q.shape[0]
    index = lax.axis_index("seq")
    barrier = pltpu.get_barrier_semaphore()

    @pl.when(index > 0)
    def _():
        pl.semaphore_signal(
            barrier, inc=1, device_id={"seq": index - 1}, device_id_type=pl.DeviceIdType.MESH
        )

    loads = {}
    order = [
        ("decay", decay_hbm, log_decay),
        ("beta", beta_hbm, beta_logit),
        ("z", lin_z_hbm, lin_z),
        ("taps_k", conv_k_hbm, conv_k),
        ("k", lin_k_hbm, lin_k),
        ("taps_v", conv_v_hbm, conv_v),
        ("v", lin_v_hbm, lin_v),
        ("taps_q", conv_q_hbm, conv_q),
        ("q", lin_q_hbm, lin_q),
        ("query", attn_query_hbm, attn_query),
        ("gate", attn_gate_hbm, attn_gate),
    ]
    for slot, (name, source, target) in enumerate(order):
        loads[name] = pltpu.make_async_copy(source, target, load_sem.at[slot])
        loads[name].start()

    def transfer(source, target, slot):
        return pltpu.make_async_remote_copy(
            src_ref=source,
            dst_ref=target,
            send_sem=send_sem.at[slot],
            recv_sem=recv_sem.at[slot],
            device_id={"seq": index + 1},
            device_id_type=pl.DeviceIdType.MESH,
        )

    tail = pl.ds(rows - rim, rim)
    early = [
        transfer(lin_k_hbm.at[tail, :], rim_k, 0),
        transfer(lin_v_hbm.at[tail, :], rim_v, 1),
        transfer(lin_q_hbm.at[tail, :], rim_q, 2),
        transfer(kv_own, kv_before, 3),
    ]
    per_group = len(pairs) // GROUPS
    states = []
    for g in range(GROUPS):
        part = pl.ds(g * 2 * per_group, 2 * per_group)
        states.append(transfer(state_out.at[part], state_in.at[part], 4 + g))

    @pl.when(index < count - 1)
    def _():
        pl.semaphore_wait(barrier, 1)
        for copy in early:
            copy.start()

    @pl.when(index == 0)
    def _():
        rim_q[...] = jnp.zeros_like(rim_q)
        rim_k[...] = jnp.zeros_like(rim_k)
        rim_v[...] = jnp.zeros_like(rim_v)
        kv_before[...] = jnp.zeros_like(kv_before)
        state_in[...] = jnp.zeros_like(state_in)

    def arrived(*copies):
        @pl.when(index > 0)
        def _():
            for copy in copies:
                copy.wait_recv()

    first = index * rows
    offsets = [jnp.int32(0)]
    for d in range(docs - 1):
        offsets.append(offsets[-1] + doc_ref[d])

    def segments(position):
        total = jnp.zeros(position.shape, jnp.int32)
        for offset in offsets:
            total = total + jnp.where(position >= offset, 1, 0)
        return total

    square = (rows, rows)
    row_id = lax.broadcasted_iota(jnp.int32, square, 0)
    col_id = lax.broadcasted_iota(jnp.int32, square, 1)
    row_seg = segments(row_id + first)
    col_seg = segments(col_id + first)
    before_seg = segments(col_id + (first - rows))
    visible = (row_id >= col_id) & (row_seg == col_seg)
    visible_before = row_seg == before_seg
    strict = row_id > col_id
    same = [None] + [
        jnp.where(row_seg == segments(row_id + (first - s)), 1.0, 0.0) for s in (1, 2, 3)
    ]
    short_seg = segments(lax.broadcasted_iota(jnp.int32, (heads, rows), 1) + first)
    last_seg = segments(jnp.full((heads, rows), rows - 1, jnp.int32) + first)
    prior_seg = segments(jnp.zeros((heads, rows), jnp.int32) + (first - 1))

    loads["decay"].wait()
    loads["beta"].wait()
    rates = log_decay[...]
    beta = jax.nn.sigmoid(beta_logit[...])
    part_a = rates.astype(BF)
    rest = rates - part_a.astype(F32)
    part_b = rest.astype(BF)
    part_c = (rest - part_b.astype(F32)).astype(BF)
    upper = jnp.where(row_id <= col_id, 1.0, 0.0).astype(BF)
    summed = mm(part_a, upper) + mm(part_b, upper) + mm(part_c, upper)
    carried_row = jnp.where(short_seg == prior_seg, jnp.exp(summed), 0.0)
    ending = jnp.where(
        short_seg == last_seg, jnp.exp(summed[:, rows - 1 : rows] - summed), 0.0
    )
    columns = jnp.concatenate(
        [
            summed,
            carried_row,
            beta * ending,
            jnp.zeros((rows - 3 * heads, rows), F32),
        ],
        axis=0,
    ).T
    carried = [columns[:, heads + h : heads + h + 1] for h in range(heads)]
    closing = [columns[:, 2 * heads + h : 2 * heads + h + 1] for h in range(heads)]

    def decays(h):
        gap = columns[:, h : h + 1] - summed[h : h + 1, :]
        return jnp.exp(jnp.where(visible, gap, NEGATIVE)) * beta[h : h + 1, :]

    def conv(values, spread, rim_ref, taps, at):
        width = pl.ds(at * LANES, LANES)
        spread[0:8, width] = rim_ref[rim - 8 : rim, width].astype(F32)
        spread[8 : 8 + rows, width] = values[:, width].astype(F32)
        total = spread[8 : 8 + rows, width] * taps[3:4, width].astype(F32)
        for s in (1, 2, 3):
            total = total + spread[8 - s : 8 - s + rows, width] * taps[
                3 - s : 4 - s, width
            ].astype(F32) * same[s]
        return total / (1.0 + jnp.exp(-total))

    def unit(x):
        return x * lax.rsqrt(jnp.sum(x * x, axis=1, keepdims=True) + 1e-06)

    loads["z"].wait()
    for h in range(heads):
        gate = lin_z[:, pl.ds(h * DV, DV)].astype(F32)
        gates[h] = gate / (1.0 + jnp.exp(-gate))
    for name in ("taps_k", "k", "taps_v", "v"):
        loads[name].wait()
    arrived(*early[:2])

    def make_states(pairs):
        for p in pairs:
            keys[p] = unit(conv(lin_k, spread_k, rim_k, conv_k, p))
        for p in pairs:
            key_high[p], key_low[p] = halves(keys[p])
            key_right[p] = jnp.concatenate([key_high[p], key_high[p], key_low[p]], axis=1)
        lower = {}
        for p in pairs:
            product = mm(
                jnp.concatenate([key_high[p], key_low[p], key_high[p]], axis=1),
                key_right[p],
                transposed=True,
            )
            product = jnp.where(strict, product, 0.0)
            for h in (2 * p, 2 * p + 1):
                decay[h] = decays(h)
            lower[p] = jnp.concatenate(
                [decay[2 * p] * product, decay[2 * p + 1] * product], axis=1
            )
        base = 8
        near = twice((row_id // base) == (col_id // base))
        eye = twice(jnp.where(row_id == col_id, 1.0, 0.0))
        power = {p: jnp.where(near, -lower[p], 0.0).astype(BF) for p in pairs}
        whole = {p: power[p].astype(F32) for p in pairs}
        power = {p: mm(power[p], block_diagonal(power[p])).astype(BF) for p in pairs}
        for p in pairs:
            both = mm(
                jnp.concatenate([power[p], whole[p].astype(BF)], axis=0), block_diagonal(power[p])
            )
            whole[p] = whole[p] + power[p].astype(F32) + both[rows:]
            power[p] = both[:rows].astype(BF)
        inverse = {
            p: eye
            + whole[p]
            + power[p].astype(F32)
            + mm(whole[p].astype(BF), block_diagonal(power[p]))
            for p in pairs
        }
        size = base
        while size < rows:
            joint = twice(
                ((row_id // (2 * size)) == (col_id // (2 * size)))
                & ((row_id // size) != (col_id // size))
            )
            short = {p: inverse[p].astype(BF) for p in pairs}
            middle = {
                p: mm(short[p], block_diagonal(jnp.where(joint, lower[p], 0.0).astype(BF))).astype(BF)
                for p in pairs
            }
            for p in pairs:
                inverse[p] = inverse[p] - mm(middle[p], block_diagonal(short[p]))
            size *= 2
        corrector, right, split_lower = {}, {}, {}
        members = [2 * p + half for p in pairs for half in range(2)]
        for p in pairs:
            corrector_pair = (inverse[p] - eye).astype(BF)
            high, low = halves(lower[p])
            for half in range(2):
                h = 2 * p + half
                lanes = slice(half * LANES, (half + 1) * LANES)
                corrector[h] = corrector_pair[:, lanes]
                split_lower[h] = jnp.concatenate([high[:, lanes], low[:, lanes]], axis=1)
                right[h] = jnp.concatenate(
                    [conv(lin_v, spread_v, rim_v, conv_v, h), carried[h] * keys[p]], axis=1
                )
        for h in members:
            solved[h] = (right[h] + mm(corrector[h], right[h].astype(BF))).astype(BF)
        for h in members:
            right[h] = (
                right[h]
                - solved[h].astype(F32)
                - mm(split_lower[h], jnp.concatenate([solved[h], solved[h]], axis=0))
            )
        for h in members:
            refined[h] = (right[h] + mm(corrector[h], right[h].astype(BF))).astype(BF)
        for p in pairs:
            parts = [
                closing[h] * (solved[h][:, :DV].astype(F32) + refined[h][:, :DV].astype(F32))
                for h in (2 * p, 2 * p + 1)
            ]
            wide = jnp.concatenate(parts, axis=1).astype(BF)
            high, low = halves(keys[p].T)
            made = mm(
                jnp.concatenate([high, low], axis=1), jnp.concatenate([wide, wide], axis=0)
            ).astype(BF)
            state_out[2 * p] = made[:, :DV]
            state_out[2 * p + 1] = made[:, DV:]

    keys, key_high, key_low, key_right, decay = {}, {}, {}, {}, {}
    solved, refined = {}, {}
    for g in range(GROUPS):
        make_states(pairs[g * per_group : (g + 1) * per_group])

        @pl.when(index < count - 1)
        def _(g=g):
            states[g].start()

    arrived(early[2], early[3])
    for name in ("taps_q", "q", "query", "gate"):
        loads[name].wait()

    for p in pairs:
        query = unit(conv(lin_q, spread_q, rim_q, conv_q, p)) * DK ** (-0.5)
        high, low = halves(query)
        product = mm(jnp.concatenate([high, low, high], axis=1), key_right[p], transposed=True)
        for h in (2 * p, 2 * p + 1):
            high, low = halves(decay[h] * product)
            mixed = mm(
                jnp.concatenate([high, low], axis=1),
                jnp.concatenate([solved[h], solved[h]], axis=0),
            ) + mm(high, refined[h])
            local_out[h] = mixed[:, :DV]
            high, low = halves(carried[h] * query - mixed[:, DV:])
            reach_out[h] = jnp.concatenate([high, low], axis=1)

    score_scale = AD ** (-0.5)
    allowed = jnp.concatenate([visible_before, visible], axis=1)
    all_keys = jnp.concatenate([kv_before[:, 0:AD], kv_own[:, 0:AD]], axis=0)
    all_values = jnp.concatenate([kv_before[:, AD:], kv_own[:, AD:]], axis=0)
    for a in range(attn_query.shape[1] // AD):
        width = pl.ds(a * AD, AD)
        scores = mm(attn_query[:, width], all_keys, transposed=True) * score_scale
        masked = jnp.where(allowed, scores, NEGATIVE)
        top = jnp.max(masked, axis=1, keepdims=True)
        weights = jnp.where(allowed, jnp.exp(masked - top), 0.0)
        total = jnp.sum(weights, axis=1, keepdims=True)
        mixture = mm(weights.astype(BF), all_values)
        gate = attn_gate[:, width].astype(F32)
        attn_out[:, width] = (mixture * (1.0 / total) / (1.0 + jnp.exp(-gate))).astype(BF)

    for h in range(heads):
        if h % (2 * per_group) == 0:
            arrived(states[h // (2 * per_group)])
        state = state_in[h]
        value = local_out[h] + mm(reach_out[h], jnp.concatenate([state, state], axis=0))
        scale = lax.rsqrt(jnp.mean(value * value, axis=1, keepdims=True) + 1e-06)
        delta_out[:, pl.ds(h * DV, DV)] = (value * scale * gates[h]).astype(BF)

    @pl.when(index < count - 1)
    def _():
        for copy in early + states:
            copy.wait_send()


def fused(
    lin_q,
    lin_k,
    lin_v,
    conv_q,
    conv_k,
    conv_v,
    lin_z,
    beta_logit,
    log_decay,
    attn_query,
    attn_gate,
    attn_kv,
    doc_lengths,
):
    rows = lin_q.shape[0]
    heads = lin_v.shape[1] // DV
    aq_local = attn_query.shape[1] // AD
    kv_head = lax.axis_index("head") * aq_local // (AQ // KVH)
    own_pair = lax.dynamic_index_in_dim(attn_kv, kv_head, axis=2, keepdims=False)
    own_pair = own_pair.reshape(rows, 2 * AD)
    streamed = (
        lin_q,
        lin_k,
        lin_v,
        conv_q,
        conv_k,
        conv_v,
        lin_z,
        beta_logit.T,
        log_decay.T,
        attn_query,
        attn_gate,
    )
    vmem = pl.BlockSpec(memory_space=pltpu.VMEM)
    rim = 16
    return pl.pallas_call(
        functools.partial(fused_kernel, lax.axis_size("seq")),
        out_shape=(
            jax.ShapeDtypeStruct(lin_z.shape, BF),
            jax.ShapeDtypeStruct(attn_query.shape, BF),
        ),
        in_specs=[pl.BlockSpec(memory_space=pltpu.SMEM), vmem]
        + [pl.BlockSpec(memory_space=pltpu.HBM)] * len(streamed),
        out_specs=(vmem, vmem),
        scratch_shapes=[pltpu.VMEM(x.shape, x.dtype) for x in streamed]
        + [
            pltpu.VMEM((rim, lin_q.shape[1]), BF),
            pltpu.VMEM((rim, lin_k.shape[1]), BF),
            pltpu.VMEM((rim, lin_v.shape[1]), BF),
            pltpu.VMEM(own_pair.shape, BF),
            pltpu.VMEM((heads, DK, DV), BF),
            pltpu.VMEM((heads, DK, DV), BF),
            pltpu.VMEM((rows + 8, lin_q.shape[1]), F32),
            pltpu.VMEM((rows + 8, lin_k.shape[1]), F32),
            pltpu.VMEM((rows + 8, lin_v.shape[1]), F32),
            pltpu.VMEM((heads, rows, DV), F32),
            pltpu.VMEM((heads, rows, 2 * DK), BF),
            pltpu.VMEM((heads, rows, DV), F32),
            pltpu.SemaphoreType.DMA((4 + GROUPS,)),
            pltpu.SemaphoreType.DMA((4 + GROUPS,)),
            pltpu.SemaphoreType.DMA((len(streamed),)),
        ],
        compiler_params=pltpu.CompilerParams(
            collective_id=0, has_side_effects=True, vmem_limit_bytes=56 * 1024 * 1024
        ),
    )(doc_lengths, own_pair, *streamed)


def solution(mesh):
    near = mesh.shape["seq"] == 4
    return jax.shard_map(
        fused if near else shards,
        mesh=mesh,
        in_specs=(
            P(("grp", "seq"), "head"),
            P(("grp", "seq"), "head"),
            P(("grp", "seq"), "head"),
            P(None, "head"),
            P(None, "head"),
            P(None, "head"),
            P(("grp", "seq"), "head"),
            P(("grp", "seq"), "head"),
            P(("grp", "seq"), "head"),
            P(("grp", "seq"), "head"),
            P(("grp", "seq"), "head"),
            P(("grp", "seq"), None, None, None),
            P("grp"),
        ),
        out_specs=(P(("grp", "seq"), "head"), P(("grp", "seq"), "head")),
        check_vma=False,
    )
```

```python
import functools

import jax
import jax.numpy as jnp
from jax import lax
from jax.experimental import pallas as pl
from jax.experimental.pallas import tpu as pltpu
from jax.sharding import PartitionSpec as P

DK = 128
DV = 128
QKH = 16
VALUE_HEADS = 32
AQ = 16
KVH = 2
AD = 256
BLOCK = 64


EXACT_PRECISION = lax.Precision.HIGHEST
NEGATIVE = -1e30


def passed_along(value, axis, steps):
    count = lax.axis_size(axis)
    initial, last = (max(0, -steps), min(count, count - steps))
    return lax.ppermute(value, axis, [(source, source + steps) for source in range(initial, last)])


def prefix_2(value, axis, combine, identity):
    length, index = (lax.axis_size(axis), lax.axis_index(axis))
    everything = jax.tree.map(
        lambda part, kind: lax.all_gather(part.astype(kind), axis),
        value,
        (jnp.bfloat16, jnp.bfloat16),
    )
    start = jax.tree.map(
        lambda part, zero: jnp.broadcast_to(jnp.asarray(zero, part.dtype), part.shape),
        value,
        identity,
    )

    def step(k, before):
        reached = k < index
        new = combine(
            before, jax.tree.map(lambda part, own: part[k].astype(own.dtype), everything, value)
        )
        return jax.tree.map(lambda a, b: jnp.where(reached, a, b), new, before)

    return lax.fori_loop(0, length, step, start)


def segment_ids(positions, doc_lengths):
    offsets = jnp.cumsum(doc_lengths) - doc_lengths
    return jnp.sum((offsets[None, :] <= positions[:, None]).astype(jnp.int32), axis=1)


def start_flags(positions, doc_lengths):
    offsets = jnp.cumsum(doc_lengths) - doc_lengths
    return jnp.any(offsets[None, :] == positions[:, None], axis=1)


def causal_conv(values, margin, weights, positions, segment, doc_lengths):
    row_count = values.shape[0]
    tap_count = weights.shape[0]
    extended = jnp.concatenate([margin, values], axis=0).astype(jnp.float32)
    conv_sum = jnp.zeros(values.shape, jnp.float32)
    for tap_index in range(tap_count):
        source = positions - (tap_count - 1) + tap_index
        inside = (segment_ids(source, doc_lengths) == segment).astype(jnp.float32)
        conv_sum = (
            conv_sum
            + extended[tap_index : tap_index + row_count]
            * weights[tap_index].astype(jnp.float32)[None, :]
            * inside[:, None]
        )
    return jax.nn.silu(conv_sum)


def unit_heads(values, head_size):
    shaped = values.reshape(values.shape[0], -1, head_size)
    return shaped * lax.rsqrt(jnp.sum(shaped * shaped, axis=-1, keepdims=True) + 1e-06)


def compose(first_pair, second_pair):
    joined_map = jnp.einsum(
        "hij,hjk->hik", second_pair[0], first_pair[0], precision=EXACT_PRECISION
    )
    joined_shift = (
        jnp.einsum("hij,hjk->hik", second_pair[0], first_pair[1], precision=EXACT_PRECISION)
        + second_pair[1]
    )
    return (joined_map, joined_shift)


def unit_lower_inverse(lower_part, block_len):
    identity = jnp.eye(block_len, dtype=jnp.float32)
    power = -lower_part
    inverse = identity + power
    for _ in range(max(block_len - 1, 1).bit_length() - 1):
        power = jnp.einsum("nhij,nhjk->nhik", power, power, precision=EXACT_PRECISION)
        inverse = jnp.einsum(
            "nhij,nhjk->nhik", inverse, identity + power, precision=EXACT_PRECISION
        )
    return inverse


def delta_blocks(queries, keys_unit, values, beta_gate, log_rates, segment, starts):
    row_count, head_count, key_size = keys_unit.shape
    value_size = values.shape[2]
    block_len = BLOCK
    block_count = row_count // block_len

    def to_blocks(array):
        return jnp.swapaxes(array.reshape((block_count, block_len) + array.shape[1:]), 1, 2)

    query_blk = to_blocks(queries)
    key_blk = to_blocks(keys_unit)
    value_blk = to_blocks(values)
    beta_blk = to_blocks(beta_gate)
    cumulative = jnp.cumsum(to_blocks(log_rates), axis=-1)
    segment_blk = segment.reshape(block_count, block_len)
    fresh_count = jnp.cumsum(starts.reshape(block_count, block_len).astype(jnp.int32), axis=-1)
    later_row = lax.broadcasted_iota(jnp.int32, (block_len, block_len), 0)
    earlier_col = lax.broadcasted_iota(jnp.int32, (block_len, block_len), 1)
    visible = (later_row >= earlier_col)[None] & (
        segment_blk[:, :, None] == segment_blk[:, None, :]
    )
    visible = visible[:, None]
    spread = cumulative[..., :, None] - cumulative[..., None, :]
    decay_mat = jnp.where(visible, jnp.exp(jnp.where(visible, spread, 0.0)), 0.0)
    carried = jnp.where((fresh_count == 0)[:, None, :], jnp.exp(cumulative), 0.0)
    key_key = jnp.einsum("nhik,nhjk->nhij", key_blk, key_blk, precision=EXACT_PRECISION)
    strict = (later_row > earlier_col).astype(jnp.float32)
    lower_part = decay_mat * strict * key_key * beta_blk[..., None, :]
    inverse = unit_lower_inverse(lower_part, block_len)
    right_side = jnp.concatenate([value_blk, carried[..., None] * key_blk], axis=-1)
    solved = jnp.einsum("nhij,nhjc->nhic", inverse, right_side, precision=EXACT_PRECISION)
    moved_values = solved[..., :value_size]
    moved_keys = solved[..., value_size:]
    query_key = jnp.einsum("nhik,nhjk->nhij", query_blk, key_blk, precision=EXACT_PRECISION)
    attend = decay_mat * query_key * beta_blk[..., None, :]
    out_zero = jnp.einsum("nhij,nhjv->nhiv", attend, moved_values, precision=EXACT_PRECISION)
    reach_part = carried[..., None] * query_blk - jnp.einsum(
        "nhij,nhjk->nhik", attend, moved_keys, precision=EXACT_PRECISION
    )
    weighted = (beta_blk * decay_mat[..., block_len - 1, :])[..., None] * key_blk
    block_map = carried[..., block_len - 1][..., None, None] * jnp.eye(
        key_size, dtype=jnp.float32
    ) - jnp.einsum("nhjk,nhjl->nhkl", weighted, moved_keys, precision=EXACT_PRECISION)
    block_shift = jnp.einsum("nhjk,nhjv->nhkv", weighted, moved_values, precision=EXACT_PRECISION)

    def advance(prefix, current):
        return (compose(prefix, current), prefix)

    eye_heads = jnp.broadcast_to(
        jnp.eye(key_size, dtype=jnp.float32), (head_count, key_size, key_size)
    )
    zero_heads = jnp.zeros((head_count, key_size, value_size), jnp.float32)
    device_pair, prefixes = lax.scan(advance, (eye_heads, zero_heads), (block_map, block_shift))
    baseline_output = out_zero + jnp.einsum(
        "nhik,nhkv->nhiv", reach_part, prefixes[1], precision=EXACT_PRECISION
    )
    complete_reach = jnp.einsum(
        "nhik,nhkl->nhil", reach_part, prefixes[0], precision=EXACT_PRECISION
    )
    return (device_pair, baseline_output, complete_reach, eye_heads, zero_heads)


def shards(
    lin_q,
    lin_k,
    lin_v,
    conv_q,
    conv_k,
    conv_v,
    lin_z,
    beta_logit,
    log_decay,
    attn_query,
    attn_gate,
    attn_kv,
    doc_lengths,
):
    row_count = lin_q.shape[0]
    seq_index = lax.axis_index("seq")
    positions = seq_index * row_count + jnp.arange(row_count, dtype=jnp.int32)
    segment = segment_ids(positions, doc_lengths)
    starts = start_flags(positions, doc_lengths)
    rim_from = row_count - conv_q.shape[0] + 1
    rim_q, rim_k, rim_v = passed_along(
        (lin_q[rim_from:], lin_k[rim_from:], lin_v[rim_from:]), "seq", 1
    )
    queries = unit_heads(
        causal_conv(lin_q, rim_q, conv_q, positions, segment, doc_lengths), DK
    ) * DK ** (-0.5)
    keys_unit = unit_heads(causal_conv(lin_k, rim_k, conv_k, positions, segment, doc_lengths), DK)
    values = causal_conv(lin_v, rim_v, conv_v, positions, segment, doc_lengths).reshape(
        row_count, -1, DV
    )
    head_count = values.shape[1]
    queries = jnp.repeat(queries, VALUE_HEADS // QKH, axis=1)
    keys_unit = jnp.repeat(keys_unit, VALUE_HEADS // QKH, axis=1)
    beta_gate = jax.nn.sigmoid(beta_logit)
    device_pair, baseline_output, complete_reach, eye_heads, zero_heads = delta_blocks(
        queries, keys_unit, values, beta_gate, log_decay, segment, starts
    )
    arriving_input = prefix_2(
        (device_pair[0], device_pair[1]), "seq", compose, (eye_heads, zero_heads)
    )
    delta_output = baseline_output + jnp.einsum(
        "dpjt,ptw->dpjw", complete_reach, arriving_input[1], precision=EXACT_PRECISION
    )
    delta_output = jnp.swapaxes(delta_output, 1, 2).reshape(row_count, head_count, DV)
    inverse_rms = lax.rsqrt(jnp.mean(delta_output * delta_output, axis=-1, keepdims=True) + 1e-06)
    gate_z = jax.nn.silu(lin_z.astype(jnp.float32).reshape(row_count, head_count, DV))
    delta_out = (
        (delta_output * inverse_rms * gate_z)
        .astype(jnp.bfloat16)
        .reshape(row_count, head_count * DV)
    )
    aq_local = attn_query.shape[1] // AD
    query_heads = attn_query.reshape(row_count, aq_local, AD)
    kv_head = lax.axis_index("head") * aq_local // (AQ // KVH)
    own_pair = lax.dynamic_index_in_dim(attn_kv, kv_head, axis=2, keepdims=False)
    score_scale = AD ** (-0.5)

    def absorb(running, kv_piece, first_row):
        row_top, row_total, accum = running
        piece_rows = kv_piece.shape[0]
        key_pos = first_row + jnp.arange(piece_rows, dtype=jnp.int32)
        key_seg = segment_ids(key_pos, doc_lengths)
        allowed = (
            (key_pos[None, :] <= positions[:, None])
            & (key_seg[None, :] == segment[:, None])
            & (key_pos[None, :] >= 0)
        )
        scores = (
            jnp.einsum(
                "qhd,kd->hqk", query_heads, kv_piece[:, 0], preferred_element_type=jnp.float32
            )
            * score_scale
        )
        masked = jnp.where(allowed[None], scores, NEGATIVE)
        new_top = jnp.maximum(row_top, jnp.max(masked, axis=-1))
        weights_f = jnp.where(allowed[None], jnp.exp(masked - new_top[..., None]), 0.0)
        rescale = jnp.exp(row_top - new_top)
        row_total = row_total * rescale + jnp.sum(weights_f, axis=-1)
        accum = accum * rescale[..., None] + jnp.einsum(
            "hqk,kd->hqd",
            weights_f.astype(jnp.bfloat16),
            kv_piece[:, 1],
            preferred_element_type=jnp.float32,
        )
        return (new_top, row_total, accum)

    start_state = (
        jnp.full((aq_local, row_count), NEGATIVE, jnp.float32),
        jnp.zeros((aq_local, row_count), jnp.float32),
        jnp.zeros((aq_local, row_count, AD), jnp.float32),
    )
    running = absorb(start_state, own_pair, seq_index * row_count)

    def hop(hop_step, loop_state):
        loop_running, kv_piece = loop_state
        kv_piece = passed_along(kv_piece, "seq", 1)
        loop_running = absorb(loop_running, kv_piece, (seq_index - hop_step - 1) * row_count)
        return (loop_running, kv_piece)

    running, _ = lax.fori_loop(0, lax.axis_size("seq") // 4, hop, (running, own_pair))
    row_top, row_total, accum = running
    attended = jnp.swapaxes(accum / row_total[..., None], 0, 1).reshape(row_count, aq_local * AD)
    attn_out = (attended * jax.nn.sigmoid(attn_gate.astype(jnp.float32))).astype(jnp.bfloat16)
    return (delta_out, attn_out)


BF = jnp.bfloat16
F32 = jnp.float32
LANES = 128
GROUPS = 2


def mm(a, b, transposed=False):
    contract = ((1,), (1,)) if transposed else ((1,), (0,))
    return lax.dot_general(a, b, (contract, ((), ())), preferred_element_type=F32)


def halves(x):
    high = x.astype(BF)
    return high, (x - high.astype(F32)).astype(BF)


def block_diagonal(wide):
    zero = jnp.zeros((wide.shape[0], LANES), wide.dtype)
    return jnp.concatenate(
        [
            jnp.concatenate([wide[:, :LANES], zero], axis=1),
            jnp.concatenate([zero, wide[:, LANES:]], axis=1),
        ],
        axis=0,
    )


def twice(x):
    return jnp.concatenate([x, x], axis=1)


def fused_kernel(
    count,
    doc_ref,
    kv_own,
    lin_q,
    lin_k,
    lin_v,
    conv_q,
    conv_k,
    conv_v,
    lin_z,
    beta_logit,
    log_decay,
    attn_query,
    attn_gate,
    delta_out,
    attn_out,
    rim_q,
    rim_k,
    rim_v,
    kv_before,
    state_out,
    state_in,
    spread_q,
    spread_k,
    spread_v,
    local_out,
    reach_out,
    gates,
    send_sem,
    recv_sem,
):
    rows = lin_q.shape[0]
    heads = lin_v.shape[1] // DV
    pairs = range(lin_k.shape[1] // DK)
    docs = doc_ref.shape[0]
    rim = rim_q.shape[0]
    index = lax.axis_index("seq")
    barrier = pltpu.get_barrier_semaphore()

    @pl.when(index > 0)
    def _():
        pl.semaphore_signal(
            barrier, inc=1, device_id={"seq": index - 1}, device_id_type=pl.DeviceIdType.MESH
        )

    def transfer(source, target, slot):
        return pltpu.make_async_remote_copy(
            src_ref=source,
            dst_ref=target,
            send_sem=send_sem.at[slot],
            recv_sem=recv_sem.at[slot],
            device_id={"seq": index + 1},
            device_id_type=pl.DeviceIdType.MESH,
        )

    tail = pl.ds(rows - rim, rim)
    early = [
        transfer(lin_k.at[tail, :], rim_k, 0),
        transfer(lin_v.at[tail, :], rim_v, 1),
        transfer(lin_q.at[tail, :], rim_q, 2),
        transfer(kv_own, kv_before, 3),
    ]
    per_group = heads // GROUPS
    states = []
    for g in range(GROUPS):
        part = pl.ds(g * per_group, per_group)
        states.append(transfer(state_out.at[part], state_in.at[part], 4 + g))

    @pl.when(index < count - 1)
    def _():
        pl.semaphore_wait(barrier, 1)
        for copy in early:
            copy.start()

    @pl.when(index == 0)
    def _():
        rim_q[...] = jnp.zeros_like(rim_q)
        rim_k[...] = jnp.zeros_like(rim_k)
        rim_v[...] = jnp.zeros_like(rim_v)
        kv_before[...] = jnp.zeros_like(kv_before)
        state_in[...] = jnp.zeros_like(state_in)

    def arrived(*copies):
        @pl.when(index > 0)
        def _():
            for copy in copies:
                copy.wait_recv()

    first = index * rows
    offsets = [jnp.int32(0)]
    for d in range(docs - 1):
        offsets.append(offsets[-1] + doc_ref[d])

    def segments(position):
        total = jnp.zeros(position.shape, jnp.int32)
        for offset in offsets:
            total = total + jnp.where(position >= offset, 1, 0)
        return total

    square = (rows, rows)
    row_id = lax.broadcasted_iota(jnp.int32, square, 0)
    col_id = lax.broadcasted_iota(jnp.int32, square, 1)
    row_seg = segments(row_id + first)
    col_seg = segments(col_id + first)
    before_seg = segments(col_id + (first - rows))
    visible = (row_id >= col_id) & (row_seg == col_seg)
    visible_before = row_seg == before_seg
    strict = row_id > col_id
    same = [None] + [
        jnp.where(row_seg == segments(row_id + (first - s)), 1.0, 0.0) for s in (1, 2, 3)
    ]
    short_seg = segments(lax.broadcasted_iota(jnp.int32, (heads, rows), 1) + first)
    last_seg = segments(jnp.full((heads, rows), rows - 1, jnp.int32) + first)
    prior_seg = segments(jnp.zeros((heads, rows), jnp.int32) + (first - 1))

    rates = log_decay[...]
    beta = jax.nn.sigmoid(beta_logit[...])
    part_a = rates.astype(BF)
    rest = rates - part_a.astype(F32)
    part_b = rest.astype(BF)
    part_c = (rest - part_b.astype(F32)).astype(BF)
    upper = jnp.where(row_id <= col_id, 1.0, 0.0).astype(BF)
    summed = mm(part_a, upper) + mm(part_b, upper) + mm(part_c, upper)
    carried_row = jnp.where(short_seg == prior_seg, jnp.exp(summed), 0.0)
    ending = jnp.where(
        short_seg == last_seg, jnp.exp(summed[:, rows - 1 : rows] - summed), 0.0
    )
    columns = jnp.concatenate(
        [
            summed,
            carried_row,
            beta * ending,
            jnp.zeros((rows - 3 * heads, rows), F32),
        ],
        axis=0,
    ).T
    carried = [columns[:, heads + h : heads + h + 1] for h in range(heads)]
    closing = [columns[:, 2 * heads + h : 2 * heads + h + 1] for h in range(heads)]

    def decays(h):
        gap = columns[:, h : h + 1] - summed[h : h + 1, :]
        return jnp.exp(jnp.where(visible, gap, NEGATIVE)) * beta[h : h + 1, :]

    def conv(values, spread, rim_ref, taps, at):
        width = pl.ds(at * LANES, LANES)
        spread[0:8, width] = rim_ref[rim - 8 : rim, width].astype(F32)
        spread[8 : 8 + rows, width] = values[:, width].astype(F32)
        total = spread[8 : 8 + rows, width] * taps[3:4, width].astype(F32)
        for s in (1, 2, 3):
            total = total + spread[8 - s : 8 - s + rows, width] * taps[
                3 - s : 4 - s, width
            ].astype(F32) * same[s]
        return total / (1.0 + jnp.exp(-total))

    def unit(x):
        return x * lax.rsqrt(jnp.sum(x * x, axis=1, keepdims=True) + 1e-06)

    arrived(*early[:2])

    keys = {p: unit(conv(lin_k, spread_k, rim_k, conv_k, p)) for p in pairs}
    key_high, key_low, key_right = {}, {}, {}
    for p in pairs:
        key_high[p], key_low[p] = halves(keys[p])
        key_right[p] = jnp.concatenate([key_high[p], key_high[p], key_low[p]], axis=1)
    lower, decay = {}, {}
    for p in pairs:
        product = mm(
            jnp.concatenate([key_high[p], key_low[p], key_high[p]], axis=1),
            key_right[p],
            transposed=True,
        )
        product = jnp.where(strict, product, 0.0)
        for h in (2 * p, 2 * p + 1):
            decay[h] = decays(h)
        lower[p] = jnp.concatenate(
            [decay[2 * p] * product, decay[2 * p + 1] * product], axis=1
        )
    base = 8
    near = twice((row_id // base) == (col_id // base))
    eye = twice(jnp.where(row_id == col_id, 1.0, 0.0))
    power = {p: jnp.where(near, -lower[p], 0.0).astype(BF) for p in pairs}
    whole = {p: power[p].astype(F32) for p in pairs}
    power = {p: mm(power[p], block_diagonal(power[p])).astype(BF) for p in pairs}
    for p in pairs:
        both = mm(
            jnp.concatenate([power[p], whole[p].astype(BF)], axis=0), block_diagonal(power[p])
        )
        whole[p] = whole[p] + power[p].astype(F32) + both[rows:]
        power[p] = both[:rows].astype(BF)
    inverse = {
        p: eye
        + whole[p]
        + power[p].astype(F32)
        + mm(whole[p].astype(BF), block_diagonal(power[p]))
        for p in pairs
    }
    size = base
    while size < rows:
        joint = twice(
            ((row_id // (2 * size)) == (col_id // (2 * size)))
            & ((row_id // size) != (col_id // size))
        )
        short = {p: inverse[p].astype(BF) for p in pairs}
        middle = {
            p: mm(short[p], block_diagonal(jnp.where(joint, lower[p], 0.0).astype(BF))).astype(BF)
            for p in pairs
        }
        for p in pairs:
            inverse[p] = inverse[p] - mm(middle[p], block_diagonal(short[p]))
        size *= 2
    corrector, solved, refined, right, split_lower = {}, {}, {}, {}, {}
    for p in pairs:
        corrector_pair = (inverse[p] - eye).astype(BF)
        high, low = halves(lower[p])
        for half in range(2):
            h = 2 * p + half
            lanes = slice(half * LANES, (half + 1) * LANES)
            corrector[h] = corrector_pair[:, lanes]
            split_lower[h] = jnp.concatenate([high[:, lanes], low[:, lanes]], axis=1)
            right[h] = jnp.concatenate(
                [conv(lin_v, spread_v, rim_v, conv_v, h), carried[h] * keys[p]], axis=1
            )
    for g in range(GROUPS):
        members = range(g * per_group, (g + 1) * per_group)
        for h in members:
            solved[h] = (right[h] + mm(corrector[h], right[h].astype(BF))).astype(BF)
        for h in members:
            right[h] = (
                right[h]
                - solved[h].astype(F32)
                - mm(split_lower[h], jnp.concatenate([solved[h], solved[h]], axis=0))
            )
        for h in members:
            refined[h] = (right[h] + mm(corrector[h], right[h].astype(BF))).astype(BF)
        for p in pairs[g * per_group // 2 : (g + 1) * per_group // 2]:
            parts = [
                closing[h] * (solved[h][:, :DV].astype(F32) + refined[h][:, :DV].astype(F32))
                for h in (2 * p, 2 * p + 1)
            ]
            wide = jnp.concatenate(parts, axis=1).astype(BF)
            high, low = halves(keys[p].T)
            made = mm(
                jnp.concatenate([high, low], axis=1), jnp.concatenate([wide, wide], axis=0)
            ).astype(BF)
            state_out[2 * p] = made[:, :DV]
            state_out[2 * p + 1] = made[:, DV:]

        @pl.when(index < count - 1)
        def _(g=g):
            states[g].start()

    arrived(early[2], early[3])

    for p in pairs:
        query = unit(conv(lin_q, spread_q, rim_q, conv_q, p)) * DK ** (-0.5)
        high, low = halves(query)
        product = mm(jnp.concatenate([high, low, high], axis=1), key_right[p], transposed=True)
        for h in (2 * p, 2 * p + 1):
            high, low = halves(decay[h] * product)
            mixed = mm(
                jnp.concatenate([high, low], axis=1),
                jnp.concatenate([solved[h], solved[h]], axis=0),
            ) + mm(high, refined[h])
            local_out[h] = mixed[:, :DV]
            high, low = halves(carried[h] * query - mixed[:, DV:])
            reach_out[h] = jnp.concatenate([high, low], axis=1)

    score_scale = AD ** (-0.5)
    allowed = jnp.concatenate([visible_before, visible], axis=1)
    all_keys = jnp.concatenate([kv_before[:, 0:AD], kv_own[:, 0:AD]], axis=0)
    all_values = jnp.concatenate([kv_before[:, AD:], kv_own[:, AD:]], axis=0)
    for a in range(attn_query.shape[1] // AD):
        width = pl.ds(a * AD, AD)
        scores = mm(attn_query[:, width], all_keys, transposed=True) * score_scale
        masked = jnp.where(allowed, scores, NEGATIVE)
        top = jnp.max(masked, axis=1, keepdims=True)
        weights = jnp.where(allowed, jnp.exp(masked - top), 0.0)
        total = jnp.sum(weights, axis=1, keepdims=True)
        mixture = mm(weights.astype(BF), all_values)
        gate = attn_gate[:, width].astype(F32)
        attn_out[:, width] = (mixture * (1.0 / total) / (1.0 + jnp.exp(-gate))).astype(BF)
    for h in range(heads):
        gate = lin_z[:, pl.ds(h * DV, DV)].astype(F32)
        gates[h] = gate / (1.0 + jnp.exp(-gate))

    for h in range(heads):
        if h % per_group == 0:
            arrived(states[h // per_group])
        state = state_in[h]
        value = local_out[h] + mm(reach_out[h], jnp.concatenate([state, state], axis=0))
        scale = lax.rsqrt(jnp.mean(value * value, axis=1, keepdims=True) + 1e-06)
        delta_out[:, pl.ds(h * DV, DV)] = (value * scale * gates[h]).astype(BF)

    @pl.when(index < count - 1)
    def _():
        for copy in early + states:
            copy.wait_send()


def fused(
    lin_q,
    lin_k,
    lin_v,
    conv_q,
    conv_k,
    conv_v,
    lin_z,
    beta_logit,
    log_decay,
    attn_query,
    attn_gate,
    attn_kv,
    doc_lengths,
):
    rows = lin_q.shape[0]
    heads = lin_v.shape[1] // DV
    aq_local = attn_query.shape[1] // AD
    kv_head = lax.axis_index("head") * aq_local // (AQ // KVH)
    own_pair = lax.dynamic_index_in_dim(attn_kv, kv_head, axis=2, keepdims=False)
    own_pair = own_pair.reshape(rows, 2 * AD)
    streamed = (
        lin_q,
        lin_k,
        lin_v,
        conv_q,
        conv_k,
        conv_v,
        lin_z,
        beta_logit.T,
        log_decay.T,
        attn_query,
        attn_gate,
    )
    vmem = pl.BlockSpec(memory_space=pltpu.VMEM)
    rim = 8
    return pl.pallas_call(
        functools.partial(fused_kernel, lax.axis_size("seq")),
        out_shape=(
            jax.ShapeDtypeStruct(lin_z.shape, BF),
            jax.ShapeDtypeStruct(attn_query.shape, BF),
        ),
        in_specs=[pl.BlockSpec(memory_space=pltpu.SMEM)] + [vmem] * 12,
        out_specs=(vmem, vmem),
        scratch_shapes=[
            pltpu.VMEM((rim, lin_q.shape[1]), BF),
            pltpu.VMEM((rim, lin_k.shape[1]), BF),
            pltpu.VMEM((rim, lin_v.shape[1]), BF),
            pltpu.VMEM(own_pair.shape, BF),
            pltpu.VMEM((heads, DK, DV), BF),
            pltpu.VMEM((heads, DK, DV), BF),
            pltpu.VMEM((rows + 8, lin_q.shape[1]), F32),
            pltpu.VMEM((rows + 8, lin_k.shape[1]), F32),
            pltpu.VMEM((rows + 8, lin_v.shape[1]), F32),
            pltpu.VMEM((heads, rows, DV), F32),
            pltpu.VMEM((heads, rows, 2 * DK), BF),
            pltpu.VMEM((heads, rows, DV), F32),
            pltpu.SemaphoreType.DMA((4 + GROUPS,)),
            pltpu.SemaphoreType.DMA((4 + GROUPS,)),
        ],
        compiler_params=pltpu.CompilerParams(
            collective_id=0, has_side_effects=True, vmem_limit_bytes=48 * 1024 * 1024
        ),
    )(doc_lengths, own_pair, *streamed)


def solution(mesh):
    near = mesh.shape["seq"] == 4
    return jax.shard_map(
        fused if near else shards,
        mesh=mesh,
        in_specs=(
            P(("grp", "seq"), "head"),
            P(("grp", "seq"), "head"),
            P(("grp", "seq"), "head"),
            P(None, "head"),
            P(None, "head"),
            P(None, "head"),
            P(("grp", "seq"), "head"),
            P(("grp", "seq"), "head"),
            P(("grp", "seq"), "head"),
            P(("grp", "seq"), "head"),
            P(("grp", "seq"), "head"),
            P(("grp", "seq"), None, None, None),
            P("grp"),
        ),
        out_specs=(P(("grp", "seq"), "head"), P(("grp", "seq"), "head")),
        check_vma=False,
    )
```
